128 devices in a mesh: dp: 4 (over y), tensor: 32 (over z, x, core).
Axes of the slice: x: 4, y: 4, z: 4, core: 2. Of those that a mesh axis runs over, the one named last changes fastest.
Arguments:
- tokens: bfloat16 [1536, 8192], P('dp', 'tensor'), may hold values from -6 to 6
- cotangent: bfloat16 [1536, 8192], P('dp', 'tensor'), may hold values from -6 to 6
- gate_weight: bfloat16 [8192, 14336], P(None, 'tensor'), may hold values from -0.125 to 0.125
- up_weight: bfloat16 [8192, 14336], P(None, 'tensor'), may hold values from -0.125 to 0.125
- down_weight: bfloat16 [14336, 8192], P('tensor'), may hold values from -0.09375 to 0.09375
- block_task: int32 [12], P('dp'), may hold values from 0 to 63
- block_fill: int32 [12], P('dp'), may hold values from 1 to 128
- task_slot: int32 [64], replicated, may hold values from 0 to 63, each once
- inner_correction_weights: bfloat16 [64, 64, 8192], P('dp', None, 'tensor'), may hold values from -0.0625 to 0.0625
- up_b: bfloat16 [64, 64, 14336], P('dp', None, 'tensor'), may hold values from -0.75 to 0.75
Outputs:
- mixed: bfloat16 [1536, 8192], P('dp', 'tensor')
- item_derivative: bfloat16 [1536, 8192], P('dp', 'tensor')
- up_a_grad: bfloat16 [64, 64, 8192], P('dp', None, 'tensor')
- up_b_grad: bfloat16 [64, 64, 14336], P('dp', None, 'tensor')
The draws below stay inside these ranges and needn't reach their ends.
Inputs may be any that keep to these rules, and one draw needn't show every extreme that they name: `task_slot`: slot s is held by data group s // 16.
All inputs are finite; a program needn't handle non-finite values.
Results may differ from the reference program's by a relative error of at most 0.019.
Values may be sent and summed in bfloat16 or wider, within the bound.
A program may use at most 128 MiB of HBM per device.

```python
import math
import jax
import jax.numpy as jnp
import numpy as np
from jax import lax

FEATURE_COUNT = 8192
HIDDEN_UNITS = 14336
R = 64
TASKS = 64
BLOCK = 128
ITEM_COUNT = 1536
BLOCKS = 12
N_TENSOR = 32


def plant(values, own_key, least, top_value):
    longest = values.shape.index(max(values.shape))
    spots = []
    for shift in (0, 1):
        where = [jax.random.randint(jax.random.fold_in(own_key, axis), (), 0, length) for axis, length in enumerate(values.shape)]
        where[longest] = (where[longest] + shift) % values.shape[longest]
        spots.append(tuple(where))
    return values.at[spots[0]].set(least).at[spots[1]].set(top_value)


def spiked(array, stream_key, source, target, blocks, factor):
    def block_of(dim):
        return (jnp.arange(array.shape[dim]) // (array.shape[dim] // blocks)).reshape((-1,) + (1,) * (array.ndim - 1 - dim))

    one_side = jax.random.permutation(stream_key, blocks)[block_of(target)]
    second = (block_of(target) + blocks // 2) % blocks
    return jnp.where((block_of(source) == one_side) | (block_of(source) == second), factor * array, array)


def steps_of(rng, shape, pieces, smallest, high):
    def one(position, blocks):
        draws = jax.random.uniform(jax.random.fold_in(jax.random.fold_in(rng, 6), position), (blocks,), jnp.float32, smallest / len(pieces), high / len(pieces))
        return jnp.repeat(jnp.exp(draws), shape[position] // blocks).reshape((-1,) + (1,) * (len(shape) - position - 1))

    factor_of = one(*pieces[0])
    for cut in pieces[1:]:
        factor_of = factor_of * one(*cut)
    return factor_of


def rank_table(number_of, skew):
    loads = [(1 << 20) // math.isqrt(grade ** skew) + 1 for grade in range(1, number_of + 1)]
    scale = 1 + sum(loads) // (1 << 30)
    return np.cumsum(np.array([max(1, weight // scale) for weight in loads]))


def ranked_ids(own_key, extent, count, slope):
    listing = rank_table(count, slope)
    ticket = jax.random.randint(jax.random.fold_in(own_key, 1), extent, 0, int(listing[count - 1]))
    grade = jnp.searchsorted(jnp.asarray(listing, jnp.int32), ticket, side="right")
    return jax.random.permutation(jax.random.fold_in(own_key, 2), count)[grade].astype(jnp.int32)


def bell_draw(stream_key, shape, deviation, reach, split=(), kind=jnp.bfloat16):
    loudness = steps_of(stream_key, shape, split, -0.22, 0.18) if split else 1.0
    entries = jax.random.normal(stream_key, shape, jnp.float32) * deviation * loudness
    return jnp.minimum(jnp.maximum(entries, -reach), reach).astype(kind)


def heavy_noise(rng, dims, deviation, most, cuts, heavy, held_as=jnp.bfloat16):
    values = deviation * jax.random.normal(rng, dims, jnp.float32)
    if cuts:
        values = values * steps_of(rng, dims, cuts, -0.22, 0.18)
    return jnp.clip(spiked(values, jax.random.fold_in(rng, 3), *heavy), -most, most).astype(held_as)


def setup_inputs(seed: int = 0) -> dict:
    key_list = jax.random.split(jax.random.key(seed), 11)
    return {
        "tokens": bell_draw(key_list[0], (ITEM_COUNT, FEATURE_COUNT), 1.0, 6.0, ((0, 4), (1, 32))),
        "cotangent": bell_draw(key_list[1], (ITEM_COUNT, FEATURE_COUNT), 1.0, 6.0, ((0, 4), (1, 32))),
        "gate_weight": heavy_noise(key_list[2], (FEATURE_COUNT, HIDDEN_UNITS), FEATURE_COUNT ** -0.5, 0.125, ((1, 32),), (1, 0, 32, 2.75)),
        "up_weight": heavy_noise(key_list[3], (FEATURE_COUNT, HIDDEN_UNITS), FEATURE_COUNT ** -0.5, 0.125, ((1, 32),), (1, 0, 32, 2.75)),
        "down_weight": heavy_noise(key_list[4], (HIDDEN_UNITS, FEATURE_COUNT), HIDDEN_UNITS ** -0.5, 0.09375, ((0, 32),), (0, 1, 32, 2.75)),
        "block_task": plant(ranked_ids(key_list[5], (BLOCKS,), TASKS, 2), jax.random.fold_in(key_list[5], 3), 0, TASKS - 1).astype(jnp.int32),
        "block_fill": plant(jax.random.randint(key_list[6], (BLOCKS,), 1, BLOCK + 1), jax.random.fold_in(key_list[6], 1), 1, BLOCK).astype(jnp.int32),
        "task_slot": jax.random.permutation(key_list[7], TASKS).astype(jnp.int32),
        "inner_correction_weights": bell_draw(key_list[8], (TASKS, R, FEATURE_COUNT), FEATURE_COUNT ** -0.5, 0.0625, ((0, 4), (2, 32))),
        "up_b": bell_draw(key_list[9], (TASKS, R, HIDDEN_UNITS), R ** -0.5, 0.75, ((0, 4), (2, 32))),
    }


adapter_scale = 0.25


def group_sum(pairs, width):
    row_total = pairs[0][0].shape[0]
    col_total = pairs[0][1].shape[1]

    def add_group(group, total):
        begin = (group * width).astype(jnp.int32)
        part = jnp.zeros((row_total, col_total), jnp.float32)
        for left, right in pairs:
            left_piece = lax.dynamic_slice_in_dim(left, begin, width, 1)
            right_piece = lax.dynamic_slice_in_dim(right, begin, width, 0)
            part = part + jnp.dot(left_piece, right_piece, preferred_element_type=jnp.float32)
        rounded = lax.optimization_barrier(part.astype(jnp.bfloat16))
        return total + rounded.astype(jnp.float32)

    return lax.fori_loop(0, N_TENSOR, add_group, jnp.zeros((row_total, col_total), jnp.float32))


def reference(tokens, cotangent, gate_weight, up_weight, down_weight, block_task, block_fill, task_slot, inner_correction_weights, up_b):
    block_count = ITEM_COUNT // BLOCK
    width = HIDDEN_UNITS // N_TENSOR
    segment_owner_index = task_slot[block_task].astype(jnp.int32)
    enabled_flags = (jnp.arange(BLOCK, dtype=jnp.int32)[None, :] < block_fill[:, None]).astype(jnp.float32)[..., None]
    portion_clusters = tokens.reshape(block_count, BLOCK, FEATURE_COUNT).astype(jnp.float32)
    correction_source_vector = inner_correction_weights[segment_owner_index].astype(jnp.float32)
    up_factor_output = up_b[segment_owner_index].astype(jnp.float32)
    gate = jnp.dot(tokens, gate_weight, preferred_element_type=jnp.float32)
    locked_raise_values = jnp.dot(tokens, up_weight, preferred_element_type=jnp.float32)
    narrow_product = jnp.einsum("imk,iok->imo", portion_clusters, correction_source_vector) * enabled_flags
    low_rank_b_output = narrow_product.astype(jnp.bfloat16)
    adapter_up_output = jnp.einsum("vam,vmk->vak", low_rank_b_output.astype(jnp.float32), up_factor_output).reshape(ITEM_COUNT, HIDDEN_UNITS)
    up_projection = locked_raise_values + adapter_scale * adapter_up_output
    sigmoid_gate = jax.nn.sigmoid(gate)
    activated = gate * sigmoid_gate
    hidden = (activated * up_projection).astype(jnp.bfloat16)
    mixed = group_sum([(hidden, down_weight)], width).astype(jnp.bfloat16)
    d_hidden = jnp.dot(cotangent, down_weight.T, preferred_element_type=jnp.float32)
    d_gate = (d_hidden * up_projection * sigmoid_gate * (1.0 + gate * (1.0 - sigmoid_gate))).astype(jnp.bfloat16)
    d_up = (d_hidden * activated).astype(jnp.bfloat16)
    gradient_per_block = d_up.reshape(block_count, BLOCK, HIDDEN_UNITS).astype(jnp.float32)
    narrow_derivative = adapter_scale * jnp.einsum("oge,oce->ogc", gradient_per_block, up_factor_output) * enabled_flags
    exterior_multiplier_dual = narrow_derivative.astype(jnp.bfloat16).astype(jnp.float32)
    fixed_weight_derivative = group_sum([(d_gate, gate_weight.T), (d_up, up_weight.T)], width)
    adjoint_of_correction = jnp.einsum("lxu,luz->lxz", exterior_multiplier_dual, correction_source_vector).reshape(ITEM_COUNT, FEATURE_COUNT)
    item_derivative = (fixed_weight_derivative + adjoint_of_correction).astype(jnp.bfloat16)
    one_hot = (segment_owner_index[:, None] == jnp.arange(TASKS, dtype=jnp.int32)[None, :]).astype(jnp.float32)
    arriving_slope = jnp.einsum("bqf,bqm->bfm", exterior_multiplier_dual, portion_clusters)
    output_gradient = adapter_scale * jnp.einsum("wvd,wvg->wdg", low_rank_b_output.astype(jnp.float32), gradient_per_block)
    up_a_grad = jnp.einsum("bs,brd->srd", one_hot, arriving_slope, precision=lax.Precision.HIGHEST).astype(jnp.bfloat16)
    up_b_grad = jnp.einsum("bs,brf->srf", one_hot, output_gradient, precision=lax.Precision.HIGHEST).astype(jnp.bfloat16)
    return mixed, item_derivative, up_a_grad, up_b_grad
```

```python
import functools

import jax
import jax.numpy as jnp
from jax import lax
from jax.experimental import pallas as pl
from jax.experimental.pallas import tpu as pltpu
from jax.sharding import PartitionSpec as P

BLOCK = 128
SIDE = 4
CHIPS = SIDE * SIDE
MESH = pl.DeviceIdType.MESH
LAG = 6

GATHER_ORDER = (0, 4, 1, 8, 2, 12, 3, 5, 6, 9, 10, 13, 7, 14, 11, 15)
SCATTER_ORDER = (15, 14, 11, 13, 7, 12, 3, 10, 9, 6, 8, 2, 5, 4, 1, 0)

adapter_scale = 0.25


def pick(table, step):
    value = jnp.int32(table[0])
    for k in range(1, len(table)):
        value = jnp.where(step == k, jnp.int32(table[k]), value)
    return value


def shifted(position, offset, sign):
    delta = jnp.where(offset == 1, -sign, 0) + jnp.where(offset == 2, sign, 0) + jnp.where(offset == 3, 2, 0)
    return lax.rem(position + delta + SIDE, SIDE)


def layer_kernel(
    tokens_ref,
    cotangent_ref,
    gate_hbm,
    up_hbm,
    down_hbm,
    extra_ref,
    mixed_ref,
    item_ref,
    d_up_ref,
    gathered,
    gate_w,
    up_w,
    down_w,
    gate_acc,
    up_acc,
    dh_acc,
    hidden,
    d_gate,
    to_partner,
    parts,
    landed,
    own_sem,
    weight_sem,
    ag_send,
    ag_recv,
    pair_send,
    pair_recv,
    half_send,
    half_recv,
    rs_send,
    rs_recv,
):
    rows, width = tokens_ref.shape
    hidden_width = gate_acc.shape[1]
    part_rows = rows // 2
    me = lax.axis_index("tensor")
    core = lax.rem(me, 2)
    x = lax.rem(me // 2, SIDE)
    z = me // (2 * SIDE)
    sign = 1 - 2 * core
    partner = me + sign

    def index(zz, xx, cc):
        return (zz * SIDE + xx) * 2 + cc

    x_up = index(z, lax.rem(x + sign + SIDE, SIDE), core)
    x_down = index(z, lax.rem(x - sign + SIDE, SIDE), core)
    z_up = index(lax.rem(z + sign + SIDE, SIDE), x, core)
    z_down = index(lax.rem(z - sign + SIDE, SIDE), x, core)
    along = {"x": (x_up, x_down), "z": (z_up, z_down)}

    def mine(idx):
        return index(shifted(z, idx % SIDE, sign), shifted(x, idx // SIDE, sign), core)

    def theirs(idx):
        return index(shifted(z, idx % SIDE, -sign), shifted(x, idx // SIDE, -sign), 1 - core)

    def remote(src, dst, send, recv, to):
        return pltpu.make_async_remote_copy(
            src_ref=src, dst_ref=dst, send_sem=send, recv_sem=recv, device_id={"tensor": to}, device_id_type=MESH
        )

    barrier = pltpu.get_barrier_semaphore()
    for peer in (partner, x_up, x_down, z_up, z_down):
        pl.semaphore_signal(barrier, inc=1, device_id={"tensor": peer}, device_id_type=MESH)

    own = [
        pltpu.make_async_copy(ref, gathered.at[a, me], own_sem.at[a])
        for a, ref in enumerate((tokens_ref, cotangent_ref))
    ]
    for copy in own:
        copy.start()

    def weight_copies(shard):
        at = pl.multiple_of(shard * width, width)
        return (
            pltpu.make_async_copy(gate_hbm.at[:, pl.ds(at, width)], gate_w.at[shard], weight_sem.at[0, shard]),
            pltpu.make_async_copy(up_hbm.at[:, pl.ds(at, width)], up_w.at[shard], weight_sem.at[1, shard]),
            pltpu.make_async_copy(down_hbm.at[:, pl.ds(at, width)], down_w.at[shard], weight_sem.at[2, shard]),
        )

    pl.semaphore_wait(barrier, 5)

    half = (slice(0, part_rows), slice(part_rows, rows))

    def ag_copy(a, h, shard, idx, to):
        ref = gathered.at[a, shard, half[h], :]
        return remote(ref, ref, ag_send.at[a, h, idx], ag_recv.at[a, h, idx], to)

    def arrive(a, idx, first):
        ox, oz = idx // SIDE, idx % SIDE
        shard = mine(idx)
        if first:
            own[a].wait()
        for h, (name_f, name_g) in enumerate((("x", "z"), ("z", "x"))):
            of, og = (ox, oz) if h == 0 else (oz, ox)

            def spot(f, g, h=h):
                return f * SIDE + g if h == 0 else g * SIDE + f

            if not first:
                ag_copy(a, h, shard, idx, x_up).wait_recv()
            f_up, f_down = along[name_f]
            g_up, g_down = along[name_g]
            if first:
                ag_copy(a, h, shard, spot(1, 0), f_up).start()
                ag_copy(a, h, shard, spot(2, 0), f_down).start()
                ag_copy(a, h, shard, spot(0, 1), g_up).start()
                ag_copy(a, h, shard, spot(0, 2), g_down).start()
            else:

                @pl.when(jnp.logical_and(og == 0, of == 1))
                def _():
                    ag_copy(a, h, shard, spot(3, 0), f_up).start()

                @pl.when(og == 0)
                def _():
                    ag_copy(a, h, shard, spot(of, 1), g_up).start()
                    ag_copy(a, h, shard, spot(of, 2), g_down).start()

                @pl.when(og == 1)
                def _():
                    ag_copy(a, h, shard, spot(of, 3), g_up).start()

        pair_copy(a, shard, idx).start()

    def pair_copy(a, shard, idx):
        ref = gathered.at[a, shard]
        return remote(ref, ref, pair_send.at[a, idx], pair_recv.at[a, idx], partner)

    arrive(0, jnp.int32(0), True)

    def start_weights(kind):
        def at_step(k, carry):
            idx = pick(GATHER_ORDER, k)
            for shard in (mine(idx), theirs(idx)):
                copies = weight_copies(shard)
                for copy in copies[:2] if kind == 0 else copies[2:]:
                    copy.start()
            return carry

        lax.fori_loop(0, CHIPS, at_step, 0)

    start_weights(0)
    start_weights(1)
    gate_acc[...] = jnp.zeros_like(gate_acc)
    up_acc[...] = jnp.zeros_like(up_acc)
    dh_acc[...] = jnp.zeros_like(dh_acc)

    across = (((1,), (1,)), ((), ()))

    def use(a, shard):
        copies = weight_copies(shard)
        if a == 0:
            copies[0].wait()
            copies[1].wait()
            piece = gathered[0, shard]
            gate_acc[...] += lax.dot_general(piece, gate_w[shard], across, preferred_element_type=jnp.float32)
            up_acc[...] += lax.dot_general(piece, up_w[shard], across, preferred_element_type=jnp.float32)
        else:
            copies[2].wait()
            dh_acc[...] += lax.dot_general(
                gathered[1, shard], down_w[shard], across, preferred_element_type=jnp.float32
            )

    def visit(a, k):
        @pl.when(jnp.logical_and(k >= 1, k < CHIPS))
        def _():
            arrive(a, pick(GATHER_ORDER, k), False)

        for which in (0, 1):

            @pl.when(k < CHIPS if which == 0 else jnp.logical_and(k >= 1, k < CHIPS + 1))
            def _():
                idx = pick(GATHER_ORDER, k - which)
                if which == 0:
                    shard = mine(idx)
                else:
                    shard = theirs(idx)
                    pair_copy(a, shard, idx).wait_recv()
                use(a, shard)

    def gather_step(k, carry):
        @pl.when(k == LAG)
        def _():
            arrive(1, jnp.int32(0), True)

        @pl.when(k < CHIPS + 1)
        def _():
            visit(0, k)

        @pl.when(k >= LAG)
        def _():
            visit(1, k - LAG)

        return carry

    lax.fori_loop(0, CHIPS + 1 + LAG, gather_step, 0)

    def middle(block, carry):
        at = pl.ds(pl.multiple_of(block * 64, 64), 64)
        gate = gate_acc[at, :]
        up = up_acc[at, :] + adapter_scale * extra_ref[at, :]
        d_hidden = dh_acc[at, :]
        sigmoid_gate = jax.nn.sigmoid(gate)
        activated = gate * sigmoid_gate
        hidden[at, :] = (activated * up).astype(jnp.bfloat16)
        d_gate[at, :] = (d_hidden * up * sigmoid_gate * (1.0 + gate * (1.0 - sigmoid_gate))).astype(jnp.bfloat16)
        d_up_ref[at, :] = (d_hidden * activated).astype(jnp.bfloat16)
        return carry

    lax.fori_loop(0, rows // 64, middle, 0)

    def product(r, shard):
        if r == 0:
            return jnp.dot(hidden[...], down_w[shard], preferred_element_type=jnp.float32)
        return jnp.dot(d_gate[...], gate_w[shard], preferred_element_type=jnp.float32) + jnp.dot(
            d_up_ref[...], up_w[shard], preferred_element_type=jnp.float32
        )

    def half_copy(r, idx):
        return remote(to_partner.at[idx], parts.at[r, idx], half_send.at[r, idx], half_recv.at[r, idx], partner)

    def rs_copy(r, h, idx, slot, to):
        return remote(parts.at[r, idx, half[h], :], landed.at[r, h, slot], rs_send.at[r, h, slot], rs_recv.at[r, h, slot], to)

    names = (("z", "x"), ("x", "z"))

    def place(h, f, g):
        return g * SIDE + f if h == 0 else f * SIDE + g

    def produce(r, k):
        @pl.when(k < CHIPS)
        def _():
            idx = pick(SCATTER_ORDER, k)
            if r == 1:
                half_copy(0, idx).wait_send()
            to_partner[idx] = product(r, theirs(idx)).astype(jnp.bfloat16)
            half_copy(r, idx).start()

        @pl.when(k >= 2)
        def _():
            idx = pick(SCATTER_ORDER, k - 2)
            half_copy(r, idx).wait_recv()
            parts[r, idx] = (product(r, mine(idx)) + parts[r, idx].astype(jnp.float32)).astype(jnp.bfloat16)
            ox, oz = idx // SIDE, idx % SIDE
            for h in (0, 1):
                of, og = (oz, ox) if h == 0 else (ox, oz)
                f_up, f_down = along[names[h][0]]

                @pl.when(of == 3)
                def _():
                    rs_copy(r, h, idx, og, f_down).start()

                @pl.when(of == 2)
                def _():
                    rs_copy(r, h, idx, SIDE + og, f_up).start()

    def add_in(r, h, idx, slots, out=None):
        for slot in slots:
            rs_copy(r, h, idx, slot, x_up).wait_recv()
        total = parts[r, idx, half[h], :].astype(jnp.float32)
        for slot in slots:
            total = total + landed[r, h, slot].astype(jnp.float32)
        if out is None:
            parts[r, idx, half[h], :] = total.astype(jnp.bfloat16)
        else:
            out[half[h], :] = total.astype(out.dtype)

    def combine(r, h, g):
        idx = place(h, 1, g)
        add_in(r, h, idx, (g,))
        rs_copy(r, h, idx, 2 * SIDE + g, along[names[h][0]][1]).start()

    def finish(r, h, g):
        idx = place(h, 0, g)
        add_in(r, h, idx, (SIDE + g, 2 * SIDE + g))
        g_up, g_down = along[names[h][1]]
        if g == 3:
            rs_copy(r, h, idx, 3 * SIDE, g_down).start()
        elif g == 2:
            rs_copy(r, h, idx, 3 * SIDE + 1, g_up).start()
        elif g == 1:
            add_in(r, h, idx, (3 * SIDE,))
            rs_copy(r, h, idx, 3 * SIDE + 2, g_down).start()
        else:
            add_in(r, h, idx, (3 * SIDE + 1, 3 * SIDE + 2), (mixed_ref, item_ref)[r])

    def mixed_step(k, carry):
        produce(0, k)
        return carry

    lax.fori_loop(0, CHIPS + 2, mixed_step, 0)

    def item_step(k, carry):
        produce(1, k)
        for n, g in enumerate((3, 2, 1, 0)):

            @pl.when(k == 1 + 2 * n)
            def _():
                combine(0, 0, g)
                combine(0, 1, g)

            @pl.when(k == 10 + 2 * n)
            def _():
                finish(0, 0, g)
                finish(0, 1, g)

        return carry

    lax.fori_loop(0, CHIPS + 2, item_step, 0)
    for g in (3, 2, 1, 0):
        combine(1, 0, g)
        combine(1, 1, g)
    for g in (3, 2, 1, 0):
        finish(1, 0, g)
        finish(1, 1, g)

    def drain(k, carry):
        for a in (0, 1):
            pair_copy(a, me, k).wait_send()

            @pl.when(k >= 1)
            def _():
                for h in (0, 1):
                    ag_copy(a, h, me, k, x_up).wait_send()

            @pl.when(k < 15)
            def _():
                for h in (0, 1):
                    rs_copy(a, h, k, k, x_up).wait_send()

        half_copy(1, k).wait_send()
        return carry

    lax.fori_loop(0, CHIPS, drain, 0)


def layer(tokens, cotangent, gate_weight, up_weight, down_weight, extra):
    rows, width = tokens.shape
    hidden_width = gate_weight.shape[1]
    shards = gate_weight.shape[0] // width
    half = rows // 2
    any_spec = pl.BlockSpec(memory_space=pl.ANY)
    vmem_spec = pl.BlockSpec(memory_space=pltpu.VMEM)
    bf16, f32 = jnp.bfloat16, jnp.float32
    dma = pltpu.SemaphoreType.DMA
    return pl.pallas_call(
        layer_kernel,
        out_shape=(
            jax.ShapeDtypeStruct((rows, width), bf16),
            jax.ShapeDtypeStruct((rows, width), f32),
            jax.ShapeDtypeStruct((rows, hidden_width), bf16),
        ),
        in_specs=[any_spec] * 5 + [vmem_spec],
        out_specs=(vmem_spec,) * 3,
        scratch_shapes=[
            pltpu.VMEM((2, shards, rows, width), bf16),
            pltpu.VMEM((shards, hidden_width, width), bf16),
            pltpu.VMEM((shards, hidden_width, width), bf16),
            pltpu.VMEM((shards, hidden_width, width), bf16),
            pltpu.VMEM((rows, hidden_width), f32),
            pltpu.VMEM((rows, hidden_width), f32),
            pltpu.VMEM((rows, hidden_width), f32),
            pltpu.VMEM((rows, hidden_width), bf16),
            pltpu.VMEM((rows, hidden_width), bf16),
            pltpu.VMEM((CHIPS, rows, width), bf16),
            pltpu.VMEM((2, CHIPS, rows, width), bf16),
            pltpu.VMEM((2, 2, 15, half, width), bf16),
            dma((2,)),
            dma((3, shards)),
            dma((2, 2, CHIPS)),
            dma((2, 2, CHIPS)),
            dma((2, CHIPS)),
            dma((2, CHIPS)),
            dma((2, CHIPS)),
            dma((2, CHIPS)),
            dma((2, 2, 15)),
            dma((2, 2, 15)),
        ],
        compiler_params=pltpu.CompilerParams(
            collective_id=0, has_side_effects=True, vmem_limit_bytes=67043328
        ),
        name="layer",
    )(tokens, cotangent, gate_weight.T, up_weight.T, down_weight, extra)


def tensor_total(value):
    return lax.psum(value.astype(jnp.bfloat16), "tensor").astype(jnp.float32)


def body(
    tokens,
    cotangent,
    gate_weight,
    up_weight,
    down_weight,
    block_task,
    block_fill,
    task_slot,
    inner_correction_weights,
    up_b,
):
    row_count, local_width = tokens.shape
    block_count = block_task.shape[0]
    hidden_width = gate_weight.shape[1]
    task_ids = jnp.arange(task_slot.shape[0], dtype=jnp.int32)
    segment_owner_index = jnp.sum(
        jnp.where(block_task[:, None] == task_ids[None, :], task_slot[None, :], 0), axis=1
    )
    enabled_flags = (jnp.arange(BLOCK, dtype=jnp.int32)[None, :] < block_fill[:, None]).astype(
        jnp.float32
    )[..., None]
    complete_arrivals, every_out = (
        lax.all_gather(inner_correction_weights, "dp", axis=0, tiled=True),
        lax.all_gather(up_b, "dp", axis=0, tiled=True),
    )
    correction_source_vector = complete_arrivals[segment_owner_index]
    up_factor_output = every_out[segment_owner_index]
    portion_clusters = tokens.reshape(block_count, BLOCK, local_width)
    narrow_product = (
        tensor_total(
            jnp.einsum(
                "imk,iok->imo",
                portion_clusters,
                correction_source_vector,
                preferred_element_type=jnp.float32,
            )
        )
        * enabled_flags
    )
    low_rank_b_output = narrow_product.astype(jnp.bfloat16)
    adapter_up_output = jnp.einsum(
        "vam,vmk->vak", low_rank_b_output, up_factor_output, preferred_element_type=jnp.float32
    ).reshape(row_count, hidden_width)
    mixed, fixed, d_up = layer(tokens, cotangent, gate_weight, up_weight, down_weight, adapter_up_output)
    gradient_per_block = d_up.reshape(block_count, BLOCK, hidden_width)
    narrow_derivative = (
        adapter_scale
        * tensor_total(
            jnp.einsum(
                "oge,oce->ogc",
                gradient_per_block,
                up_factor_output,
                preferred_element_type=jnp.float32,
            )
        )
        * enabled_flags
    )
    exterior_multiplier_dual = narrow_derivative.astype(jnp.bfloat16)
    adjoint_of_correction = jnp.einsum(
        "lxu,luz->lxz",
        exterior_multiplier_dual,
        correction_source_vector,
        preferred_element_type=jnp.float32,
    ).reshape(row_count, local_width)
    item_derivative = (fixed + adjoint_of_correction).astype(jnp.bfloat16)
    arriving_slope = jnp.einsum(
        "bqf,bqm->bfm",
        exterior_multiplier_dual,
        portion_clusters,
        preferred_element_type=jnp.float32,
    )
    output_gradient = adapter_scale * jnp.einsum(
        "wvd,wvg->wdg", low_rank_b_output, gradient_per_block, preferred_element_type=jnp.float32
    )
    slot_ids = jnp.arange(task_slot.shape[0], dtype=jnp.int32)
    one_hot = (segment_owner_index[:, None] == slot_ids[None, :]).astype(jnp.float32)
    spread_in = jnp.einsum("bs,brd->srd", one_hot, arriving_slope, precision=lax.Precision.HIGHEST)
    spread_out = jnp.einsum(
        "bs,brf->srf", one_hot, output_gradient, precision=lax.Precision.HIGHEST
    )
    owned_in, owned_out = (
        lax.psum_scatter(
            spread_in.astype(jnp.bfloat16), "dp", scatter_dimension=0, tiled=True
        ).astype(jnp.float32),
        lax.psum_scatter(
            spread_out.astype(jnp.bfloat16), "dp", scatter_dimension=0, tiled=True
        ).astype(jnp.float32),
    )
    return (mixed, item_derivative, owned_in.astype(jnp.bfloat16), owned_out.astype(jnp.bfloat16))


def solution(mesh):
    return jax.shard_map(
        body,
        mesh=mesh,
        in_specs=(
            P("dp", "tensor"),
            P("dp", "tensor"),
            P(None, "tensor"),
            P(None, "tensor"),
            P("tensor", None),
            P("dp"),
            P("dp"),
            P(),
            P("dp", None, "tensor"),
            P("dp", None, "tensor"),
        ),
        out_specs=(
            P("dp", "tensor"),
            P("dp", "tensor"),
            P("dp", None, "tensor"),
            P("dp", None, "tensor"),
        ),
        check_vma=False,
    )
```

```python
import jax
import jax.numpy as jnp
from jax import lax
from jax.experimental import pallas as pl
from jax.experimental.pallas import tpu as pltpu
from jax.sharding import PartitionSpec as P

BLOCK = 128
SIDE = 4
CHIPS = SIDE * SIDE
MESH = pl.DeviceIdType.MESH
LAG = 6

GATHER_ORDER = (0, 4, 1, 8, 2, 12, 3, 5, 6, 9, 10, 13, 7, 14, 11, 15)
SCATTER_ORDER = (15, 14, 11, 13, 7, 12, 3, 10, 9, 6, 8, 2, 5, 4, 1, 0)

adapter_scale = 0.25


def pick(table, step):
    value = jnp.int32(table[0])
    for k in range(1, len(table)):
        value = jnp.where(step == k, jnp.int32(table[k]), value)
    return value


def shifted(position, offset, sign):
    delta = jnp.where(offset == 1, -sign, 0) + jnp.where(offset == 2, sign, 0) + jnp.where(offset == 3, 2, 0)
    return lax.rem(position + delta + SIDE, SIDE)


def layer_kernel(
    tokens_ref,
    cotangent_ref,
    gate_hbm,
    up_hbm,
    down_hbm,
    task_ref,
    fill_ref,
    slot_ref,
    inner_hbm,
    up_b_hbm,
    mixed_ref,
    item_ref,
    grad_in_ref,
    grad_out_ref,
    place_ref,
    gathered,
    gate_w,
    up_w,
    down_w,
    gate_acc,
    up_acc,
    dh_acc,
    hidden,
    d_gate,
    d_up_ref,
    parts,
    landed,
    own_tokens,
    inner_own,
    up_b_own,
    task_land,
    task_smem,
    lent_in,
    lent_out,
    borrowed_in,
    borrowed_out,
    inner_rows,
    up_rows,
    partial,
    sum_out,
    sum_in,
    low,
    grads_in,
    grads_out,
    landed_in,
    landed_out,
    own_sem,
    weight_sem,
    ag_send,
    ag_recv,
    pair_send,
    pair_recv,
    half_send,
    half_recv,
    rs_send,
    rs_recv,
    task_send,
    task_recv,
    lend_send,
    lend_recv,
    sum_send,
    sum_recv,
    grad_send,
    grad_recv,
):
    rows, width = tokens_ref.shape
    blocks = rows // BLOCK
    part_rows = rows // 2
    to_partner = gathered.at[0]
    y = lax.axis_index("dp")
    owned_slots = inner_own.shape[0]
    me = lax.axis_index("tensor")
    core = lax.rem(me, 2)
    x = lax.rem(me // 2, SIDE)
    z = me // (2 * SIDE)
    sign = 1 - 2 * core
    partner = me + sign

    def index(zz, xx, cc):
        return (zz * SIDE + xx) * 2 + cc

    x_up = index(z, lax.rem(x + sign + SIDE, SIDE), core)
    x_down = index(z, lax.rem(x - sign + SIDE, SIDE), core)
    z_up = index(lax.rem(z + sign + SIDE, SIDE), x, core)
    z_down = index(lax.rem(z - sign + SIDE, SIDE), x, core)
    along = {"x": (x_up, x_down), "z": (z_up, z_down)}

    def mine(idx):
        return index(shifted(z, idx % SIDE, sign), shifted(x, idx // SIDE, sign), core)

    def theirs(idx):
        return index(shifted(z, idx % SIDE, -sign), shifted(x, idx // SIDE, -sign), 1 - core)

    def remote(src, dst, send, recv, to):
        return pltpu.make_async_remote_copy(
            src_ref=src, dst_ref=dst, send_sem=send, recv_sem=recv, device_id={"tensor": to}, device_id_type=MESH
        )

    barrier = pltpu.get_barrier_semaphore()
    x_far = index(z, lax.rem(x + 2, SIDE), core)
    z_far = index(lax.rem(z + 2, SIDE), x, core)
    for peer in (partner, x_up, x_down, z_up, z_down, x_far, z_far):
        pl.semaphore_signal(barrier, inc=1, device_id={"tensor": peer}, device_id_type=MESH)
    for d in (1, 2, 3):
        pl.semaphore_signal(barrier, inc=1, device_id={"dp": lax.rem(y + d, SIDE)}, device_id_type=MESH)

    own = [
        pltpu.make_async_copy(ref, gathered.at[a, me], own_sem.at[a])
        for a, ref in enumerate((tokens_ref, cotangent_ref))
    ]
    for copy in own:
        copy.start()
    locals_in = (
        pltpu.make_async_copy(tokens_ref, own_tokens, own_sem.at[2]),
        pltpu.make_async_copy(inner_hbm, inner_own, own_sem.at[3]),
        pltpu.make_async_copy(up_b_hbm, up_b_own, own_sem.at[4]),
        pltpu.make_async_copy(task_ref, task_smem.at[0], own_sem.at[5]),
    )
    for copy in locals_in:
        copy.start()

    def weight_copies(shard):
        at = pl.multiple_of(shard * width, width)
        return (
            pltpu.make_async_copy(gate_hbm.at[:, pl.ds(at, width)], gate_w.at[shard], weight_sem.at[0, shard]),
            pltpu.make_async_copy(up_hbm.at[:, pl.ds(at, width)], up_w.at[shard], weight_sem.at[1, shard]),
            pltpu.make_async_copy(down_hbm.at[:, pl.ds(at, width)], down_w.at[shard], weight_sem.at[2, shard]),
        )

    pl.semaphore_wait(barrier, 10)

    def dp_remote(src, dst, send, recv, d):
        return pltpu.make_async_remote_copy(
            src_ref=src,
            dst_ref=dst,
            send_sem=send,
            recv_sem=recv,
            device_id={"dp": lax.rem(y + d, SIDE)},
            device_id_type=MESH,
        )

    def task_copy(d):
        return dp_remote(task_ref, task_land.at[d - 1], task_send.at[d - 1], task_recv.at[d - 1], d)

    for d in (1, 2, 3):
        task_copy(d).start()

    half = (slice(0, part_rows), slice(part_rows, rows))

    def ag_copy(a, h, shard, idx, to):
        ref = gathered.at[a, shard, half[h], :]
        return remote(ref, ref, ag_send.at[a, h, idx], ag_recv.at[a, h, idx], to)

    def arrive(a, idx, first):
        ox, oz = idx // SIDE, idx % SIDE
        shard = mine(idx)
        if first:
            own[a].wait()
        for h, (name_f, name_g) in enumerate((("x", "z"), ("z", "x"))):
            of, og = (ox, oz) if h == 0 else (oz, ox)

            def spot(f, g, h=h):
                return f * SIDE + g if h == 0 else g * SIDE + f

            if not first:
                ag_copy(a, h, shard, idx, x_up).wait_recv()
            f_up, f_down = along[name_f]
            g_up, g_down = along[name_g]
            if first:
                ag_copy(a, h, shard, spot(1, 0), f_up).start()
                ag_copy(a, h, shard, spot(2, 0), f_down).start()
                ag_copy(a, h, shard, spot(0, 1), g_up).start()
                ag_copy(a, h, shard, spot(0, 2), g_down).start()
            else:

                @pl.when(jnp.logical_and(og == 0, of == 1))
                def _():
                    ag_copy(a, h, shard, spot(3, 0), f_up).start()

                @pl.when(og == 0)
                def _():
                    ag_copy(a, h, shard, spot(of, 1), g_up).start()
                    ag_copy(a, h, shard, spot(of, 2), g_down).start()

                @pl.when(og == 1)
                def _():
                    ag_copy(a, h, shard, spot(of, 3), g_up).start()

        pair_copy(a, shard, idx).start()

    def pair_copy(a, shard, idx):
        ref = gathered.at[a, shard]
        return remote(ref, ref, pair_send.at[a, idx], pair_recv.at[a, idx], partner)

    arrive(0, jnp.int32(0), True)

    def start_weights(kind):
        def one_step(k, carry):
            idx = pick(GATHER_ORDER, k)
            for shard in (mine(idx), theirs(idx)):
                copies = weight_copies(shard)
                for copy in copies[:2] if kind == 0 else copies[2:]:
                    copy.start()
            return carry

        lax.fori_loop(0, CHIPS, one_step, 0)

    start_weights(0)
    start_weights(1)
    gate_acc[...] = jnp.zeros_like(gate_acc)
    up_acc[...] = jnp.zeros_like(up_acc)
    dh_acc[...] = jnp.zeros_like(dh_acc)

    across = (((1,), (1,)), ((), ()))

    def lend_copy(kind, d):
        src, dst = ((lent_in, borrowed_in), (lent_out, borrowed_out))[kind]
        return dp_remote(src.at[d], dst.at[d - 1], lend_send.at[kind, d - 1], lend_recv.at[kind, d - 1], d)

    def spot_of(rank, j):
        return slot_ref[task_smem[rank, 0, j]] - owned_slots * y

    def lend():
        for d in (1, 2, 3):
            task_copy(d).wait_recv()
        to_smem = pltpu.make_async_copy(task_land, task_smem.at[pl.ds(1, 3)], own_sem.at[6])
        to_smem.start()
        for copy in locals_in:
            copy.wait()
        to_smem.wait()
        for kind, (own_ref, lent) in enumerate(((inner_own, lent_in), (up_b_own, lent_out))):
            for d in (1, 2, 3, 0):
                for j in range(blocks):
                    spot = spot_of((SIDE - d) % SIDE, j)
                    held = jnp.logical_and(spot >= 0, spot < owned_slots)
                    safe = jnp.clip(spot, 0, owned_slots - 1)
                    factor = jnp.where(held, 1.0, 0.0)
                    lent[d, j] = (own_ref[safe].astype(jnp.float32) * factor).astype(jnp.bfloat16)
                if d:
                    lend_copy(kind, d).start()
        for d in range(SIDE):
            for j in range(blocks):
                place_ref[d * blocks + j] = spot_of(d, j)

    def borrow(kind):
        lent, borrowed, held = ((lent_in, borrowed_in, inner_rows), (lent_out, borrowed_out, up_rows))[kind]
        for d in (1, 2, 3):
            lend_copy(kind, d).wait_recv()
        held[...] = lent[0] + borrowed[0] + borrowed[1] + borrowed[2]

    def block_at(b):
        return slice(b * BLOCK, (b + 1) * BLOCK)

    rank_half = partial.shape[0] // 2
    here = pl.ds(pl.multiple_of(core * rank_half, rank_half), rank_half)
    there = pl.ds(pl.multiple_of((1 - core) * rank_half, rank_half), rank_half)

    def sum_copy(w, slot, src, to):
        return remote(sum_out.at[w, src], sum_in.at[w, slot], sum_send.at[w, slot], sum_recv.at[w, slot], to)

    def sum_pair(w):
        for b in range(blocks):
            if w == 0:
                left, right = inner_rows[b], own_tokens[block_at(b), :]
            else:
                left, right = up_rows[b], d_up_ref[block_at(b), :]
            partial[:, block_at(b)] = lax.dot_general(left, right, across, preferred_element_type=jnp.float32)
        sum_out[w, 0] = partial[there, :].astype(jnp.bfloat16)
        sum_copy(w, 0, 0, partner).start()

    def sum_x(w):
        sum_copy(w, 0, 0, partner).wait_recv()
        sum_out[w, 1] = (partial[here, :] + sum_in[w, 0].astype(jnp.float32)).astype(jnp.bfloat16)
        for d in (1, 2, 3):
            sum_copy(w, d, 1, index(z, lax.rem(x + d, SIDE), core)).start()

    def sum_four(w, own_slot, first):
        total = sum_out[w, own_slot].astype(jnp.float32)
        for d in range(3):
            sum_copy(w, first + d, own_slot, partner).wait_recv()
            total = total + sum_in[w, first + d].astype(jnp.float32)
        return total.astype(jnp.bfloat16)

    def sum_z(w):
        sum_out[w, 2] = sum_four(w, 1, 1)
        for d in (1, 2, 3):
            sum_copy(w, 3 + d, 2, index(lax.rem(z + d, SIDE), x, core)).start()

    def sum_back(w):
        sum_out[w, 3] = sum_four(w, 2, 4)
        sum_copy(w, 7, 3, partner).start()

    def sum_end(w):
        sum_copy(w, 7, 3, partner).wait_recv()
        low[w, here, :] = sum_out[w, 3]
        low[w, there, :] = sum_in[w, 7]
        scale = (1.0, adapter_scale)[w]
        for b in range(blocks):
            live = lax.broadcasted_iota(jnp.int32, (2 * rank_half, BLOCK), 1) < fill_ref[b]
            value = low[w, :, block_at(b)].astype(jnp.float32)
            low[w, :, block_at(b)] = (scale * jnp.where(live, value, 0.0)).astype(jnp.bfloat16)

    def grad_copy(kind, d):
        src, dst = ((grads_in, landed_in), (grads_out, landed_out))[kind]
        return dp_remote(src, dst.at[d - 1], grad_send.at[kind, d - 1], grad_recv.at[kind, d - 1], d)

    def gradients(kind):
        for b in range(blocks):
            if kind == 0:
                grads_in[b] = jnp.dot(
                    low[1, :, block_at(b)], own_tokens[block_at(b), :], preferred_element_type=jnp.float32
                ).astype(jnp.bfloat16)
            else:
                grads_out[b] = (
                    adapter_scale
                    * jnp.dot(low[0, :, block_at(b)], d_up_ref[block_at(b), :], preferred_element_type=jnp.float32)
                ).astype(jnp.bfloat16)
        for d in (1, 2, 3):
            grad_copy(kind, d).start()

    down_rank = (((0,), (0,)), ((), ()))

    def adjoint():
        for b in range(blocks):
            gate_acc[block_at(b), 0:width] = lax.dot_general(
                low[1, :, block_at(b)], inner_rows[b], down_rank, preferred_element_type=jnp.float32
            )

    def use(a, shard):
        copies = weight_copies(shard)
        if a == 0:
            copies[0].wait()
            copies[1].wait()
            piece = gathered[0, shard]
            gate_acc[...] += lax.dot_general(piece, gate_w[shard], across, preferred_element_type=jnp.float32)
            up_acc[...] += lax.dot_general(piece, up_w[shard], across, preferred_element_type=jnp.float32)
        else:
            copies[2].wait()
            dh_acc[...] += lax.dot_general(
                gathered[1, shard], down_w[shard], across, preferred_element_type=jnp.float32
            )

    def visit(a, k):
        @pl.when(jnp.logical_and(k >= 1, k < CHIPS))
        def _():
            arrive(a, pick(GATHER_ORDER, k), False)

        for which in (0, 1):

            @pl.when(k < CHIPS if which == 0 else jnp.logical_and(k >= 1, k < CHIPS + 1))
            def _():
                idx = pick(GATHER_ORDER, k - which)
                if which == 0:
                    shard = mine(idx)
                else:
                    shard = theirs(idx)
                    pair_copy(a, shard, idx).wait_recv()
                use(a, shard)

    def at_step(k, step, do, *given):
        @pl.when(k == step)
        def _():
            do(*given)

    def gather_step(k, carry):
        @pl.when(k == LAG)
        def _():
            arrive(1, jnp.int32(0), True)

        at_step(k, 1, lend)
        at_step(k, 5, borrow, 0)
        at_step(k, 5, sum_pair, 0)
        at_step(k, 7, sum_x, 0)
        at_step(k, 10, sum_z, 0)
        at_step(k, 14, sum_back, 0)
        at_step(k, 17, sum_end, 0)
        at_step(k, 18, borrow, 1)

        @pl.when(k < CHIPS + 1)
        def _():
            visit(0, k)

        @pl.when(k >= LAG)
        def _():
            visit(1, k - LAG)

        return carry

    lax.fori_loop(0, CHIPS + 1 + LAG, gather_step, 0)

    for b in range(blocks):
        up_acc[block_at(b), :] += adapter_scale * lax.dot_general(
            low[0, :, block_at(b)], up_rows[b], down_rank, preferred_element_type=jnp.float32
        )

    def middle(block, carry):
        at = pl.ds(pl.multiple_of(block * 64, 64), 64)
        gate = gate_acc[at, :]
        up = up_acc[at, :]
        d_hidden = dh_acc[at, :]
        sigmoid_gate = jax.nn.sigmoid(gate)
        activated = gate * sigmoid_gate
        hidden[at, :] = (activated * up).astype(jnp.bfloat16)
        d_gate[at, :] = (d_hidden * up * sigmoid_gate * (1.0 + gate * (1.0 - sigmoid_gate))).astype(jnp.bfloat16)
        d_up_ref[at, :] = (d_hidden * activated).astype(jnp.bfloat16)
        return carry

    lax.fori_loop(0, rows // 64, middle, 0)
    sum_pair(1)

    def drain_tokens(k, carry):
        pair_copy(0, me, k).wait_send()

        @pl.when(k >= 1)
        def _():
            for h in (0, 1):
                ag_copy(0, h, me, k, x_up).wait_send()

        return carry

    lax.fori_loop(0, CHIPS, drain_tokens, 0)

    def product(r, shard):
        if r == 0:
            return jnp.dot(hidden[...], down_w[shard], preferred_element_type=jnp.float32)
        return jnp.dot(d_gate[...], gate_w[shard], preferred_element_type=jnp.float32) + jnp.dot(
            d_up_ref[...], up_w[shard], preferred_element_type=jnp.float32
        )

    def half_copy(r, idx):
        return remote(to_partner.at[idx], parts.at[r, idx], half_send.at[r, idx], half_recv.at[r, idx], partner)

    def rs_copy(r, h, idx, slot, to):
        return remote(parts.at[r, idx, half[h], :], landed.at[r, h, slot], rs_send.at[r, h, slot], rs_recv.at[r, h, slot], to)

    names = (("z", "x"), ("x", "z"))

    def place(h, f, g):
        return g * SIDE + f if h == 0 else f * SIDE + g

    def produce(r, k):
        @pl.when(k < CHIPS)
        def _():
            idx = pick(SCATTER_ORDER, k)
            if r == 1:
                half_copy(0, idx).wait_send()
            to_partner[idx] = product(r, theirs(idx)).astype(jnp.bfloat16)
            half_copy(r, idx).start()

        @pl.when(k >= 2)
        def _():
            idx = pick(SCATTER_ORDER, k - 2)
            half_copy(r, idx).wait_recv()
            parts[r, idx] = (product(r, mine(idx)) + parts[r, idx].astype(jnp.float32)).astype(jnp.bfloat16)
            ox, oz = idx // SIDE, idx % SIDE
            for h in (0, 1):
                of, og = (oz, ox) if h == 0 else (ox, oz)
                f_up, f_down = along[names[h][0]]

                @pl.when(of == 3)
                def _():
                    rs_copy(r, h, idx, og, f_down).start()

                @pl.when(of == 2)
                def _():
                    rs_copy(r, h, idx, SIDE + og, f_up).start()

    def add_in(r, h, idx, slots, out=None):
        for slot in slots:
            rs_copy(r, h, idx, slot, x_up).wait_recv()
        total = parts[r, idx, half[h], :].astype(jnp.float32)
        for slot in slots:
            total = total + landed[r, h, slot].astype(jnp.float32)
        if out is item_ref:
            total = total + gate_acc[half[h], 0:width]
        if out is None:
            parts[r, idx, half[h], :] = total.astype(jnp.bfloat16)
        else:
            out[half[h], :] = total.astype(out.dtype)

    def combine(r, h, g):
        idx = place(h, 1, g)
        add_in(r, h, idx, (g,))
        rs_copy(r, h, idx, 2 * SIDE + g, along[names[h][0]][1]).start()

    def finish(r, h, g):
        idx = place(h, 0, g)
        add_in(r, h, idx, (SIDE + g, 2 * SIDE + g))
        g_up, g_down = along[names[h][1]]
        if g == 3:
            rs_copy(r, h, idx, 3 * SIDE, g_down).start()
        elif g == 2:
            rs_copy(r, h, idx, 3 * SIDE + 1, g_up).start()
        elif g == 1:
            add_in(r, h, idx, (3 * SIDE,))
            rs_copy(r, h, idx, 3 * SIDE + 2, g_down).start()
        else:
            add_in(r, h, idx, (3 * SIDE + 1, 3 * SIDE + 2), (mixed_ref, item_ref)[r])

    def mixed_step(k, carry):
        produce(0, k)
        at_step(k, 1, gradients, 1)
        at_step(k, 3, sum_x, 1)
        at_step(k, 7, sum_z, 1)
        at_step(k, 11, sum_back, 1)
        at_step(k, 14, sum_end, 1)
        at_step(k, 15, gradients, 0)
        at_step(k, 16, adjoint)
        return carry

    lax.fori_loop(0, CHIPS + 2, mixed_step, 0)

    def item_step(k, carry):
        produce(1, k)
        for n, g in enumerate((3, 2, 1, 0)):

            @pl.when(k == 1 + 2 * n)
            def _():
                combine(0, 0, g)
                combine(0, 1, g)

            @pl.when(k == 10 + 2 * n)
            def _():
                finish(0, 0, g)
                finish(0, 1, g)

        return carry

    lax.fori_loop(0, CHIPS + 2, item_step, 0)
    for g in (3, 2, 1, 0):
        combine(1, 0, g)
        combine(1, 1, g)
    for g in (3, 2, 1, 0):
        finish(1, 0, g)
        finish(1, 1, g)

    grad_in_ref[0:blocks] = grads_in[...]
    grad_out_ref[0:blocks] = grads_out[...]
    for d in (1, 2, 3):
        grad_copy(0, d).wait_recv()
        grad_copy(1, d).wait_recv()
        grad_in_ref[d * blocks : (d + 1) * blocks] = landed_in[d - 1]
        grad_out_ref[d * blocks : (d + 1) * blocks] = landed_out[d - 1]
    for d in (1, 2, 3):
        task_copy(d).wait_send()
        for kind in (0, 1):
            lend_copy(kind, d).wait_send()
            grad_copy(kind, d).wait_send()
    for w in (0, 1):
        for slot, src in enumerate((0, 1, 1, 1, 2, 2, 2, 3)):
            sum_copy(w, slot, src, partner).wait_send()

    def drain(k, carry):
        pair_copy(1, me, k).wait_send()

        @pl.when(k >= 1)
        def _():
            for h in (0, 1):
                ag_copy(1, h, me, k, x_up).wait_send()

        for a in (0, 1):

            @pl.when(k < 15)
            def _():
                for h in (0, 1):
                    rs_copy(a, h, k, k, x_up).wait_send()

        half_copy(1, k).wait_send()
        return carry

    lax.fori_loop(0, CHIPS, drain, 0)


def layer(
    tokens, cotangent, gate_weight, up_weight, down_weight, block_task, block_fill, task_slot, inner, up_b
):
    rows, width = tokens.shape
    hidden_width = gate_weight.shape[1]
    shards = gate_weight.shape[0] // width
    half = rows // 2
    blocks = rows // BLOCK
    owned, rank, _ = inner.shape
    any_spec = pl.BlockSpec(memory_space=pl.ANY)
    vmem_spec = pl.BlockSpec(memory_space=pltpu.VMEM)
    smem_spec = pl.BlockSpec(memory_space=pltpu.SMEM)
    bf16, f32 = jnp.bfloat16, jnp.float32
    dma = pltpu.SemaphoreType.DMA
    tasks = jnp.broadcast_to(jnp.pad(block_task, (0, 128 - blocks))[None, :], (8, 128))
    return pl.pallas_call(
        layer_kernel,
        out_shape=(
            jax.ShapeDtypeStruct((rows, width), bf16),
            jax.ShapeDtypeStruct((rows, width), bf16),
            jax.ShapeDtypeStruct((SIDE * blocks, rank, width), bf16),
            jax.ShapeDtypeStruct((SIDE * blocks, rank, hidden_width), bf16),
            jax.ShapeDtypeStruct((SIDE * blocks,), jnp.int32),
        ),
        in_specs=[any_spec] * 5 + [vmem_spec, smem_spec, smem_spec, any_spec, any_spec],
        out_specs=(vmem_spec,) * 4 + (smem_spec,),
        scratch_shapes=[
            pltpu.VMEM((2, shards, rows, width), bf16),
            pltpu.VMEM((shards, hidden_width, width), bf16),
            pltpu.VMEM((shards, hidden_width, width), bf16),
            pltpu.VMEM((shards, hidden_width, width), bf16),
            pltpu.VMEM((rows, hidden_width), f32),
            pltpu.VMEM((rows, hidden_width), f32),
            pltpu.VMEM((rows, hidden_width), f32),
            pltpu.VMEM((rows, hidden_width), bf16),
            pltpu.VMEM((rows, hidden_width), bf16),
            pltpu.VMEM((rows, hidden_width), bf16),
            pltpu.VMEM((2, CHIPS, rows, width), bf16),
            pltpu.VMEM((2, 2, 15, half, width), bf16),
            pltpu.VMEM((rows, width), bf16),
            pltpu.VMEM((owned, rank, width), bf16),
            pltpu.VMEM((owned, rank, hidden_width), bf16),
            pltpu.VMEM((3, 8, 128), jnp.int32),
            pltpu.SMEM((SIDE, 8, 128), jnp.int32),
            pltpu.VMEM((SIDE, blocks, rank, width), bf16),
            pltpu.VMEM((SIDE, blocks, rank, hidden_width), bf16),
            pltpu.VMEM((3, blocks, rank, width), bf16),
            pltpu.VMEM((3, blocks, rank, hidden_width), bf16),
            pltpu.VMEM((blocks, rank, width), bf16),
            pltpu.VMEM((blocks, rank, hidden_width), bf16),
            pltpu.VMEM((rank, rows), f32),
            pltpu.VMEM((2, 4, rank // 2, rows), bf16),
            pltpu.VMEM((2, 8, rank // 2, rows), bf16),
            pltpu.VMEM((2, rank, rows), bf16),
            pltpu.VMEM((blocks, rank, width), bf16),
            pltpu.VMEM((blocks, rank, hidden_width), bf16),
            pltpu.VMEM((3, blocks, rank, width), bf16),
            pltpu.VMEM((3, blocks, rank, hidden_width), bf16),
            dma((7,)),
            dma((3, shards)),
            dma((2, 2, CHIPS)),
            dma((2, 2, CHIPS)),
            dma((2, CHIPS)),
            dma((2, CHIPS)),
            dma((2, CHIPS)),
            dma((2, CHIPS)),
            dma((2, 2, 15)),
            dma((2, 2, 15)),
            dma((3,)),
            dma((3,)),
            dma((2, 3)),
            dma((2, 3)),
            dma((2, 8)),
            dma((2, 8)),
            dma((2, 3)),
            dma((2, 3)),
        ],
        compiler_params=pltpu.CompilerParams(
            collective_id=0, has_side_effects=True, vmem_limit_bytes=67043328
        ),
        name="layer",
    )(
        tokens,
        cotangent,
        gate_weight.T,
        up_weight.T,
        down_weight,
        tasks,
        block_fill,
        task_slot,
        inner,
        up_b,
    )


def spread_kernel(place_ref, mixed_in, item_in, grads_in, grads_out, mixed, item, owned_in, owned_out, sum_in, sum_out):
    mixed[...] = mixed_in[...]
    item[...] = item_in[...]
    for grads, total, owned in ((grads_in, sum_in, owned_in), (grads_out, sum_out, owned_out)):
        total[...] = jnp.zeros_like(total)

        @pl.loop(0, grads.shape[0])
        def _(b):
            spot = place_ref[b]

            @pl.when(jnp.logical_and(spot >= 0, spot < total.shape[0]))
            def _():
                total[spot] += grads[b].astype(jnp.float32)

        owned[...] = total[...].astype(jnp.bfloat16)


def spread(place, mixed, item, grads_in, grads_out, owned):
    vmem_spec = pl.BlockSpec(memory_space=pltpu.VMEM)
    shapes = [(owned,) + g.shape[1:] for g in (grads_in, grads_out)]
    return pl.pallas_call(
        spread_kernel,
        out_shape=tuple(
            jax.ShapeDtypeStruct(s, jnp.bfloat16) for s in (mixed.shape, item.shape, *shapes)
        ),
        in_specs=[pl.BlockSpec(memory_space=pltpu.SMEM)] + [vmem_spec] * 4,
        out_specs=(vmem_spec,) * 4,
        scratch_shapes=[pltpu.VMEM(s, jnp.float32) for s in shapes],
        name="spread",
    )(place, mixed, item, grads_in, grads_out)


def body(
    tokens,
    cotangent,
    gate_weight,
    up_weight,
    down_weight,
    block_task,
    block_fill,
    task_slot,
    inner_correction_weights,
    up_b,
):
    mixed, item, grads_in, grads_out, place = layer(
        tokens,
        cotangent,
        gate_weight,
        up_weight,
        down_weight,
        block_task,
        block_fill,
        task_slot,
        inner_correction_weights,
        up_b,
    )
    return spread(place, mixed, item, grads_in, grads_out, up_b.shape[0])


def solution(mesh):
    return jax.shard_map(
        body,
        mesh=mesh,
        in_specs=(
            P("dp", "tensor"),
            P("dp", "tensor"),
            P(None, "tensor"),
            P(None, "tensor"),
            P("tensor", None),
            P("dp"),
            P("dp"),
            P(),
            P("dp", None, "tensor"),
            P("dp", None, "tensor"),
        ),
        out_specs=(
            P("dp", "tensor"),
            P("dp", "tensor"),
            P("dp", None, "tensor"),
            P("dp", None, "tensor"),
        ),
        check_vma=False,
    )
```

```python
import functools

import jax
import jax.numpy as jnp
from jax import lax
from jax.experimental import pallas as pl
from jax.experimental.pallas import tpu as pltpu
from jax.sharding import PartitionSpec as P

BLOCK = 128
SIDE = 4
CHIPS = SIDE * SIDE
MESH = pl.DeviceIdType.MESH
COT_SEND = 5
COT = 6
LEND = 0
LOW = 5
HIDE = 18
MIX = 18
ITEM = 24
BEHIND = 3
COMBINE = ((19, 17, 16, 14), (17, 15, 14, 11))
FINISH = ((22, 21, 20, 18), (19, 18, 17, 14))

GATHER_ORDER = (0, 4, 1, 8, 2, 12, 3, 5, 6, 10, 9, 13, 7, 14, 11, 15)
SCATTER_ORDER = (15, 14, 11, 13, 7, 12, 3, 10, 9, 5, 6, 8, 2, 4, 1, 0)

adapter_scale = 0.25


def packed(values, bits):
    word = sum(v << (bits * n) for n, v in enumerate(values))
    return jnp.int32(word - (1 << 32) if word >= 1 << 31 else word)


def pick(table, step):
    word = jnp.where(step < 8, packed(table[:8], 4), packed(table[8:], 4))
    return (word >> (4 * (step & 7))) & 15


def shifted(position, offset, sign):
    deltas = jnp.where(sign > 0, packed((0, 3, 1, 2), 2), packed((0, 1, 3, 2), 2))
    return (position + (deltas >> (2 * offset))) & 3


def timed(k, events):
    if not events:
        return
    steps = [e[0] for e in events]
    if steps[0] == steps[-1]:

        @pl.when(k == steps[0])
        def _():
            for _, do in events:
                do()

        return
    middle = steps[len(steps) // 2]
    if middle == steps[0]:
        middle = next(n for n in steps if n > middle)

    @pl.when(k < middle)
    def _():
        timed(k, [e for e in events if e[0] < middle])

    @pl.when(k >= middle)
    def _():
        timed(k, [e for e in events if e[0] >= middle])


def layer_kernel(
    tokens_ref,
    cotangent_ref,
    gate_hbm,
    up_hbm,
    down_hbm,
    task_ref,
    fill_ref,
    slot_ref,
    inner_hbm,
    up_b_hbm,
    mixed_ref,
    item_ref,
    grad_in_ref,
    grad_out_ref,
    place_ref,
    gathered,
    gate_up_w,
    down_w,
    gate_up,
    slope,
    dh_acc,
    hidden,
    d_both,
    d_up_ref,
    made,
    parts,
    landed,
    own_tokens,
    inner_own,
    up_b_own,
    task_tile,
    task_land,
    task_smem,
    lent_in,
    lent_out,
    borrowed_in,
    borrowed_out,
    inner_rows,
    up_rows,
    partial,
    sum_out,
    sum_in,
    low,
    grads_in,
    grads_out,
    landed_in,
    landed_out,
    own_sem,
    weight_sem,
    ag_send,
    ag_recv,
    pair_send,
    pair_recv,
    half_send,
    half_recv,
    rs_send,
    rs_recv,
    task_send,
    task_recv,
    lend_send,
    lend_recv,
    sum_send,
    sum_recv,
    grad_send,
    grad_recv,
    out_sem,
):
    rows, width = tokens_ref.shape
    blocks = rows // BLOCK
    part_rows = rows // 2
    hidden_width = hidden.shape[1]
    y = lax.axis_index("dp")
    owned_slots = inner_own.shape[0]
    me = lax.axis_index("tensor")
    core = me & 1
    x = (me >> 1) & 3
    z = me >> 3
    sign = 1 - 2 * core
    partner = me + sign

    here_columns = pl.ds(pl.multiple_of(core * width, width), width)
    there_columns = pl.ds(pl.multiple_of((1 - core) * width, width), width)
    my_chip = me >> 1

    def index(zz, xx, cc):
        return (zz * SIDE + xx) * 2 + cc

    x_up = index(z, (x + sign + SIDE) & 3, core)
    x_down = index(z, (x - sign + SIDE) & 3, core)
    z_up = index((z + sign + SIDE) & 3, x, core)
    z_down = index((z - sign + SIDE) & 3, x, core)
    along = {"x": (x_up, x_down), "z": (z_up, z_down)}

    def mine(idx):
        return shifted(z, idx & 3, sign) * SIDE + shifted(x, idx >> 2, sign)

    def theirs(idx):
        return shifted(z, idx & 3, -sign) * SIDE + shifted(x, idx >> 2, -sign)

    def remote(src, dst, send, recv, to):
        return pltpu.make_async_remote_copy(
            src_ref=src, dst_ref=dst, send_sem=send, recv_sem=recv, device_id={"tensor": to}, device_id_type=MESH
        )

    barrier = pltpu.get_barrier_semaphore()
    x_far = index(z, (x + 2) & 3, core)
    z_far = index((z + 2) & 3, x, core)
    for peer in (partner, x_up, x_down, z_up, z_down, x_far, z_far):
        pl.semaphore_signal(barrier, inc=1, device_id={"tensor": peer}, device_id_type=MESH)
    for d in (1, 2, 3):
        pl.semaphore_signal(barrier, inc=1, device_id={"dp": (y + d) & 3}, device_id_type=MESH)

    own = [
        pltpu.make_async_copy(ref, gathered.at[a, my_chip, :, here_columns], own_sem.at[a])
        for a, ref in enumerate((tokens_ref, cotangent_ref))
    ]
    for copy in own:
        copy.start()
    locals_in = (
        pltpu.make_async_copy(tokens_ref, own_tokens, own_sem.at[2]),
        pltpu.make_async_copy(inner_hbm, inner_own, own_sem.at[3]),
        pltpu.make_async_copy(up_b_hbm, up_b_own, own_sem.at[4]),
    )
    for copy in locals_in:
        copy.start()

    gate_part, up_part = slice(0, hidden_width), slice(hidden_width, 2 * hidden_width)

    def weight_copies(chip):
        at = pl.ds(pl.multiple_of(chip * 2 * width, 2 * width), 2 * width)
        return (
            pltpu.make_async_copy(gate_hbm.at[:, at], gate_up_w.at[chip, gate_part, :], weight_sem.at[0, chip]),
            pltpu.make_async_copy(up_hbm.at[:, at], gate_up_w.at[chip, up_part, :], weight_sem.at[1, chip]),
            pltpu.make_async_copy(down_hbm.at[:, at], down_w.at[chip], weight_sem.at[2, chip]),
        )

    lanes = lax.broadcasted_iota(jnp.int32, task_tile.shape, 1)
    tile = jnp.zeros(task_tile.shape, jnp.int32)
    for j in range(blocks):
        tile = jnp.where(lanes == j, task_ref[j], tile)
    task_tile[...] = tile

    pl.semaphore_wait(barrier, 10)

    def dp_remote(src, dst, send, recv, d):
        return pltpu.make_async_remote_copy(
            src_ref=src,
            dst_ref=dst,
            send_sem=send,
            recv_sem=recv,
            device_id={"dp": (y + d) & 3},
            device_id_type=MESH,
        )

    def task_copy(d):
        return dp_remote(task_tile, task_land.at[d - 1], task_send.at[d - 1], task_recv.at[d - 1], d)

    for d in (1, 2, 3):
        task_copy(d).start()

    half = (slice(0, part_rows), slice(part_rows, rows))

    def ag_copy(a, h, chip, idx, to):
        ref = gathered.at[a, chip, half[h], here_columns]
        return remote(ref, ref, ag_send.at[a, h, idx], ag_recv.at[a, h, idx], to)

    def arrive(a, idx, first):
        ox, oz = idx >> 2, idx & 3
        chip = mine(idx)
        if first:
            own[a].wait()
        for h, (name_f, name_g) in enumerate((("x", "z"), ("z", "x"))):
            of, og = (ox, oz) if h == 0 else (oz, ox)

            def spot(f, g, h=h):
                return f * SIDE + g if h == 0 else g * SIDE + f

            if not first:
                ag_copy(a, h, chip, idx, x_up).wait_recv()
            f_up, f_down = along[name_f]
            g_up, g_down = along[name_g]
            if first:
                ag_copy(a, h, chip, spot(1, 0), f_up).start()
                ag_copy(a, h, chip, spot(2, 0), f_down).start()
                ag_copy(a, h, chip, spot(0, 1), g_up).start()
                ag_copy(a, h, chip, spot(0, 2), g_down).start()
            else:

                @pl.when(jnp.logical_and(og == 0, of == 1))
                def _():
                    ag_copy(a, h, chip, spot(3, 0), f_up).start()

                @pl.when(og == 0)
                def _():
                    ag_copy(a, h, chip, spot(of, 1), g_up).start()
                    ag_copy(a, h, chip, spot(of, 2), g_down).start()

                @pl.when(og == 1)
                def _():
                    ag_copy(a, h, chip, spot(of, 3), g_up).start()

        pair_copy(a, chip, idx, here_columns).start()

    def pair_copy(a, chip, idx, columns):
        ref = gathered.at[a, chip, :, columns]
        return remote(ref, ref, pair_send.at[a, idx], pair_recv.at[a, idx], partner)

    arrive(0, jnp.int32(0), True)

    def start_weights(k, carry):
        for copy in weight_copies(mine(pick(GATHER_ORDER, k))):
            copy.start()
        return carry

    lax.fori_loop(0, CHIPS, start_weights, 0)
    gate_up[...] = jnp.zeros_like(gate_up)
    dh_acc[...] = jnp.zeros_like(dh_acc)

    across = (((1,), (1,)), ((), ()))

    def lend_copy(kind, d):
        src, dst = ((lent_in, borrowed_in), (lent_out, borrowed_out))[kind]
        return dp_remote(src.at[d], dst.at[d - 1], lend_send.at[kind, d - 1], lend_recv.at[kind, d - 1], d)

    def spot_of(rank, j):
        task = task_smem[rank - 1, 0, j] if rank else task_ref[j]
        return slot_ref[task] - owned_slots * y

    def lend():
        for d in (1, 2, 3):
            task_copy(d).wait_recv()
        to_smem = pltpu.make_async_copy(task_land, task_smem, own_sem.at[5])
        to_smem.start()
        for copy in locals_in:
            copy.wait()
        to_smem.wait()
        for kind, (own_ref, lent) in enumerate(((inner_own, lent_in), (up_b_own, lent_out))):
            for d in (1, 2, 3, 0):
                for j in range(blocks):
                    spot = spot_of((SIDE - d) % SIDE, j)
                    held = jnp.logical_and(spot >= 0, spot < owned_slots)
                    safe = jnp.clip(spot, 0, owned_slots - 1)
                    factor = jnp.where(held, 1.0, 0.0)
                    lent[d, j] = (own_ref[safe].astype(jnp.float32) * factor).astype(jnp.bfloat16)
                if d:
                    lend_copy(kind, d).start()
        for d in range(SIDE):
            for j in range(blocks):
                place_ref[d * blocks + j] = spot_of(d, j)

    def borrow(kind):
        lent, borrowed, held = ((lent_in, borrowed_in, inner_rows), (lent_out, borrowed_out, up_rows))[kind]
        for d in (1, 2, 3):
            lend_copy(kind, d).wait_recv()
        held[...] = lent[0] + borrowed[0] + borrowed[1] + borrowed[2]

    def block_at(b):
        return slice(b * BLOCK, (b + 1) * BLOCK)

    rank_half = partial.shape[0] // 2
    here = pl.ds(pl.multiple_of(core * rank_half, rank_half), rank_half)
    there = pl.ds(pl.multiple_of((1 - core) * rank_half, rank_half), rank_half)

    def sum_copy(w, slot, src, to):
        return remote(sum_out.at[w, src], sum_in.at[w, slot], sum_send.at[w, slot], sum_recv.at[w, slot], to)

    def sum_pair(w):
        for b in range(blocks):
            if w == 0:
                left, right = inner_rows[b], own_tokens[block_at(b), :]
            else:
                left, right = up_rows[b], d_up_ref[block_at(b), :]
            partial[:, block_at(b)] = lax.dot_general(left, right, across, preferred_element_type=jnp.float32)
        sum_out[w, 0] = partial[there, :].astype(jnp.bfloat16)
        sum_copy(w, 0, 0, partner).start()

    def sum_x(w):
        sum_copy(w, 0, 0, partner).wait_recv()
        sum_out[w, 1] = (partial[here, :] + sum_in[w, 0].astype(jnp.float32)).astype(jnp.bfloat16)
        for d in (1, 2, 3):
            sum_copy(w, d, 1, index(z, (x + d) & 3, core)).start()

    def sum_four(w, own_slot, first):
        total = sum_out[w, own_slot].astype(jnp.float32)
        for d in range(3):
            sum_copy(w, first + d, own_slot, partner).wait_recv()
            total = total + sum_in[w, first + d].astype(jnp.float32)
        return total.astype(jnp.bfloat16)

    def sum_z(w):
        sum_out[w, 2] = sum_four(w, 1, 1)
        for d in (1, 2, 3):
            sum_copy(w, 3 + d, 2, index((z + d) & 3, x, core)).start()

    def sum_back(w):
        sum_out[w, 3] = sum_four(w, 2, 4)
        sum_copy(w, 7, 3, partner).start()

    def sum_end(w):
        sum_copy(w, 7, 3, partner).wait_recv()
        low[w, here, :] = sum_out[w, 3]
        low[w, there, :] = sum_in[w, 7]
        scale = (1.0, adapter_scale)[w]
        for b in range(blocks):
            live = lax.broadcasted_iota(jnp.int32, (2 * rank_half, BLOCK), 1) < fill_ref[b]
            value = low[w, :, block_at(b)].astype(jnp.float32)
            low[w, :, block_at(b)] = (scale * jnp.where(live, value, 0.0)).astype(jnp.bfloat16)

    def grad_copy(kind, d):
        src, dst = ((grads_in, landed_in), (grads_out, landed_out))[kind]
        return dp_remote(src, dst.at[d - 1], grad_send.at[kind, d - 1], grad_recv.at[kind, d - 1], d)

    def gradients(kind):
        for b in range(blocks):
            if kind == 0:
                grads_in[b] = jnp.dot(
                    low[1, :, block_at(b)], own_tokens[block_at(b), :], preferred_element_type=jnp.float32
                ).astype(jnp.bfloat16)
            else:
                grads_out[b] = (
                    adapter_scale
                    * jnp.dot(low[0, :, block_at(b)], d_up_ref[block_at(b), :], preferred_element_type=jnp.float32)
                ).astype(jnp.bfloat16)
        for d in (1, 2, 3):
            grad_copy(kind, d).start()
        out_copy(kind, 0).start()

    def out_copy(kind, d):
        ref, own_grads, landed_grads = ((grad_in_ref, grads_in, landed_in), (grad_out_ref, grads_out, landed_out))[kind]
        src = landed_grads.at[d - 1] if d else own_grads
        return pltpu.make_async_copy(src, ref.at[pl.ds(d * blocks, blocks)], out_sem.at[kind, d])

    def collect():
        for kind in (1, 0):
            for d in (1, 2, 3):
                grad_copy(kind, d).wait_recv()
                out_copy(kind, d).start()

    down_rank = (((0,), (0,)), ((), ()))

    def adjoint():
        for b in range(blocks):
            gate_up[block_at(b), 0:width] = lax.dot_general(
                low[1, :, block_at(b)], inner_rows[b], down_rank, preferred_element_type=jnp.float32
            )

    def use(a, chip):
        if a == 0:
            for copy in weight_copies(chip):
                copy.wait()
        total, weights = ((gate_up, gate_up_w), (dh_acc, down_w))[a]
        total[...] += lax.dot_general(
            gathered[a, chip], weights[chip], across, preferred_element_type=jnp.float32
        )

    def visit(a, k):
        @pl.when(jnp.logical_and(k >= 1, k < CHIPS))
        def _():
            arrive(a, pick(GATHER_ORDER, k), False)

        @pl.when(jnp.logical_and(k >= 1, k < CHIPS + 1))
        def _():
            idx = pick(GATHER_ORDER, k - 1)
            pair_copy(a, theirs(idx), idx, there_columns).wait_recv()

        @pl.when(k >= BEHIND)
        def _():
            use(a, mine(pick(GATHER_ORDER, k - BEHIND)))

    def hide():
        for b in range(blocks):
            slope[block_at(b), :] = adapter_scale * lax.dot_general(
                low[0, :, block_at(b)], up_rows[b], down_rank, preferred_element_type=jnp.float32
            )

        def some_rows(n, carry):
            at = pl.ds(pl.multiple_of(n * 64, 64), 64)
            gate = gate_up[at, gate_part]
            up = gate_up[at, up_part] + slope[at, :]
            sigmoid_gate = jax.nn.sigmoid(gate)
            activated = gate * sigmoid_gate
            hidden[at, :] = (activated * up).astype(jnp.bfloat16)
            gate_up[at, gate_part] = activated
            slope[at, :] = up * sigmoid_gate * (1.0 + gate * (1.0 - sigmoid_gate))
            return carry

        lax.fori_loop(0, rows // 64, some_rows, 0)

    def differentiate():
        def some_rows(n, carry):
            at = pl.ds(pl.multiple_of(n * 64, 64), 64)
            d_hidden = dh_acc[at, :]
            d_up = (d_hidden * gate_up[at, gate_part]).astype(jnp.bfloat16)
            d_both[at, gate_part] = (d_hidden * slope[at, :]).astype(jnp.bfloat16)
            d_both[at, up_part] = d_up
            d_up_ref[at, :] = d_up
            return carry

        lax.fori_loop(0, rows // 64, some_rows, 0)

    def product(r, chip):
        left, right = ((hidden, down_w), (d_both, gate_up_w))[r]
        return jnp.dot(left[...], right[chip], preferred_element_type=jnp.float32).astype(jnp.bfloat16)

    def mirrored(idx):
        swap = packed((0, 2, 1, 3), 2)
        return ((swap >> (2 * (idx >> 2))) & 3) * SIDE + ((swap >> (2 * (idx & 3))) & 3)

    def half_copy(r, slot, idx):
        to = mirrored(idx)
        return remote(
            made.at[r, slot, :, there_columns], parts.at[r, to], half_send.at[r, idx], half_recv.at[r, to], partner
        )

    def half_landed(r, idx):
        return remote(
            made.at[r, 0, :, there_columns], parts.at[r, idx], half_send.at[r, idx], half_recv.at[r, idx], partner
        )

    def rs_copy(r, h, idx, slot, to):
        return remote(parts.at[r, idx, half[h], :], landed.at[r, h, slot], rs_send.at[r, h, slot], rs_recv.at[r, h, slot], to)

    names = (("z", "x"), ("x", "z"))

    def place(h, f, g):
        return g * SIDE + f if h == 0 else f * SIDE + g

    def produce(r, k):
        @pl.when(k < CHIPS)
        def _():
            idx = pick(SCATTER_ORDER, k)
            slot = k & 3

            @pl.when(k >= 4)
            def _():
                half_copy(r, slot, pick(SCATTER_ORDER, k - 4)).wait_send()

            made[r, slot] = product(r, mine(idx))
            half_copy(r, slot, idx).start()

        @pl.when(k >= BEHIND)
        def _():
            idx = pick(SCATTER_ORDER, k - BEHIND)
            half_landed(r, idx).wait_recv()
            own_part = made[r, (k - BEHIND) & 3, :, here_columns].astype(jnp.float32)
            parts[r, idx] = (own_part + parts[r, idx].astype(jnp.float32)).astype(jnp.bfloat16)
            ox, oz = idx >> 2, idx & 3
            for h in (0, 1):
                of, og = (oz, ox) if h == 0 else (ox, oz)
                f_up, f_down = along[names[h][0]]

                @pl.when(of == 3)
                def _():
                    rs_copy(r, h, idx, og, f_down).start()

                @pl.when(of == 2)
                def _():
                    rs_copy(r, h, idx, SIDE + og, f_up).start()

    def add_in(r, h, idx, slots, out=None):
        for slot in slots:
            rs_copy(r, h, idx, slot, x_up).wait_recv()
        total = parts[r, idx, half[h], :].astype(jnp.float32)
        for slot in slots:
            total = total + landed[r, h, slot].astype(jnp.float32)
        if out is item_ref:
            total = total + gate_up[half[h], 0:width]
        if out is None:
            parts[r, idx, half[h], :] = total.astype(jnp.bfloat16)
        else:
            out[half[h], :] = total.astype(out.dtype)

    def combine(r, h, g):
        idx = place(h, 1, g)
        add_in(r, h, idx, (g,))
        rs_copy(r, h, idx, 2 * SIDE + g, along[names[h][0]][1]).start()

    def finish(r, h, g):
        idx = place(h, 0, g)
        add_in(r, h, idx, (SIDE + g, 2 * SIDE + g))
        g_up, g_down = along[names[h][1]]
        if g == 3:
            rs_copy(r, h, idx, 3 * SIDE, g_down).start()
        elif g == 2:
            rs_copy(r, h, idx, 3 * SIDE + 1, g_up).start()
        elif g == 1:
            add_in(r, h, idx, (3 * SIDE,))
            rs_copy(r, h, idx, 3 * SIDE + 2, g_down).start()
        else:
            add_in(r, h, idx, (3 * SIDE + 1, 3 * SIDE + 2), (mixed_ref, item_ref)[r])

    def both_halves(do, r, g):
        do(r, 0, g)
        do(r, 1, g)

    early = [
        (COT_SEND, lambda: arrive(1, jnp.int32(0), True)),
        (LEND, lend),
        (LOW, lambda: borrow(0)),
        (LOW, lambda: sum_pair(0)),
        (LOW + 2, lambda: sum_x(0)),
        (LOW + 5, lambda: sum_z(0)),
        (LOW + 8, lambda: sum_back(0)),
        (HIDE, lambda: borrow(1)),
        (HIDE, lambda: sum_end(0)),
        (HIDE, hide),
        (ITEM, differentiate),
        (ITEM + 1, lambda: sum_pair(1)),
        (ITEM + 1, lambda: gradients(1)),
        (ITEM + 3, lambda: sum_x(1)),
        (ITEM + 6, lambda: sum_z(1)),
        (ITEM + 9, lambda: sum_back(1)),
        (ITEM + 12, lambda: sum_end(1)),
        (ITEM + 12, lambda: gradients(0)),
        (ITEM + 13, adjoint),
        (ITEM + FINISH[1][1], collect),
    ]
    late = []
    for r, start in ((0, MIX), (1, ITEM)):
        for g in (3, 2, 1, 0):
            late.append((start + COMBINE[r][g], functools.partial(both_halves, combine, r, g)))
            late.append((start + FINISH[r][g], functools.partial(both_halves, finish, r, g)))
    early.sort(key=lambda e: e[0])
    late.sort(key=lambda e: e[0])

    def step(k, carry):
        @pl.when(k < COT + CHIPS + BEHIND)
        def _():
            for a, start in ((0, 0), (1, COT)):

                @pl.when(jnp.logical_and(k >= start, k < start + CHIPS + BEHIND))
                def _():
                    visit(a, k - start)

        timed(k, early)

        @pl.when(k >= MIX)
        def _():
            for r, start in ((0, MIX), (1, ITEM)):

                @pl.when(jnp.logical_and(k >= start, k < start + CHIPS + BEHIND))
                def _():
                    produce(r, k - start)

            timed(k, late)

        return carry

    lax.fori_loop(0, ITEM + FINISH[1][0] + 1, step, 0)
    for d in (1, 2, 3):
        task_copy(d).wait_send()
        for kind in (0, 1):
            lend_copy(kind, d).wait_send()
            grad_copy(kind, d).wait_send()
    for w in (0, 1):
        for slot, src in enumerate((0, 1, 1, 1, 2, 2, 2, 3)):
            sum_copy(w, slot, src, partner).wait_send()

    for kind in (0, 1):
        for d in range(SIDE):
            out_copy(kind, d).wait()
    for r in (0, 1):
        for k in range(CHIPS - 4, CHIPS):
            half_landed(r, SCATTER_ORDER[k]).wait_send()

    def drain(k, carry):
        for a in (0, 1):
            pair_copy(a, my_chip, k, here_columns).wait_send()

            @pl.when(k >= 1)
            def _():
                for h in (0, 1):
                    ag_copy(a, h, my_chip, k, x_up).wait_send()

            @pl.when(k < 15)
            def _():
                for h in (0, 1):
                    rs_copy(a, h, k, k, x_up).wait_send()

        return carry

    lax.fori_loop(0, CHIPS, drain, 0)


def layer(
    tokens, cotangent, gate_weight, up_weight, down_weight, block_task, block_fill, task_slot, inner, up_b
):
    rows, width = tokens.shape
    hidden_width = gate_weight.shape[1]
    half = rows // 2
    blocks = rows // BLOCK
    owned, rank, _ = inner.shape
    any_spec = pl.BlockSpec(memory_space=pl.ANY)
    vmem_spec = pl.BlockSpec(memory_space=pltpu.VMEM)
    smem_spec = pl.BlockSpec(memory_space=pltpu.SMEM)
    bf16, f32 = jnp.bfloat16, jnp.float32
    dma = pltpu.SemaphoreType.DMA
    return pl.pallas_call(
        layer_kernel,
        out_shape=(
            jax.ShapeDtypeStruct((rows, width), bf16),
            jax.ShapeDtypeStruct((rows, width), bf16),
            jax.ShapeDtypeStruct((SIDE * blocks, rank, width), bf16),
            jax.ShapeDtypeStruct((SIDE * blocks, rank, hidden_width), bf16),
            jax.ShapeDtypeStruct((SIDE * blocks,), jnp.int32),
        ),
        in_specs=[any_spec] * 5 + [smem_spec] * 3 + [any_spec] * 2,
        out_specs=(vmem_spec, vmem_spec, any_spec, any_spec, smem_spec),
        scratch_shapes=[
            pltpu.VMEM((2, CHIPS, rows, 2 * width), bf16),
            pltpu.VMEM((CHIPS, 2 * hidden_width, 2 * width), bf16),
            pltpu.VMEM((CHIPS, hidden_width, 2 * width), bf16),
            pltpu.VMEM((rows, 2 * hidden_width), f32),
            pltpu.VMEM((rows, hidden_width), f32),
            pltpu.VMEM((rows, hidden_width), f32),
            pltpu.VMEM((rows, hidden_width), bf16),
            pltpu.VMEM((rows, 2 * hidden_width), bf16),
            pltpu.VMEM((rows, hidden_width), bf16),
            pltpu.VMEM((2, 4, rows, 2 * width), bf16),
            pltpu.VMEM((2, CHIPS, rows, width), bf16),
            pltpu.VMEM((2, 2, 15, half, width), bf16),
            pltpu.VMEM((rows, width), bf16),
            pltpu.VMEM((owned, rank, width), bf16),
            pltpu.VMEM((owned, rank, hidden_width), bf16),
            pltpu.VMEM((8, 128), jnp.int32),
            pltpu.VMEM((3, 8, 128), jnp.int32),
            pltpu.SMEM((3, 8, 128), jnp.int32),
            pltpu.VMEM((SIDE, blocks, rank, width), bf16),
            pltpu.VMEM((SIDE, blocks, rank, hidden_width), bf16),
            pltpu.VMEM((3, blocks, rank, width), bf16),
            pltpu.VMEM((3, blocks, rank, hidden_width), bf16),
            pltpu.VMEM((blocks, rank, width), bf16),
            pltpu.VMEM((blocks, rank, hidden_width), bf16),
            pltpu.VMEM((rank, rows), f32),
            pltpu.VMEM((2, 4, rank // 2, rows), bf16),
            pltpu.VMEM((2, 8, rank // 2, rows), bf16),
            pltpu.VMEM((2, rank, rows), bf16),
            pltpu.VMEM((blocks, rank, width), bf16),
            pltpu.VMEM((blocks, rank, hidden_width), bf16),
            pltpu.VMEM((3, blocks, rank, width), bf16),
            pltpu.VMEM((3, blocks, rank, hidden_width), bf16),
            dma((6,)),
            dma((3, CHIPS)),
            dma((2, 2, CHIPS)),
            dma((2, 2, CHIPS)),
            dma((2, CHIPS)),
            dma((2, CHIPS)),
            dma((2, CHIPS)),
            dma((2, CHIPS)),
            dma((2, 2, 15)),
            dma((2, 2, 15)),
            dma((3,)),
            dma((3,)),
            dma((2, 3)),
            dma((2, 3)),
            dma((2, 8)),
            dma((2, 8)),
            dma((2, 3)),
            dma((2, 3)),
            dma((2, SIDE)),
        ],
        compiler_params=pltpu.CompilerParams(
            collective_id=0, has_side_effects=True, vmem_limit_bytes=67043328
        ),
        name="layer",
    )(
        tokens,
        cotangent,
        gate_weight.T,
        up_weight.T,
        down_weight,
        block_task,
        block_fill,
        task_slot,
        inner,
        up_b,
    )


def spread_kernel(place_ref, mixed_in, item_in, grads_in, grads_out, mixed, item, owned_in, owned_out, sum_in, sum_out):
    mixed[...] = mixed_in[...]
    item[...] = item_in[...]
    for grads, total, owned in ((grads_in, sum_in, owned_in), (grads_out, sum_out, owned_out)):
        total[...] = jnp.zeros_like(total)

        @pl.loop(0, grads.shape[0])
        def _(b):
            spot = place_ref[b]

            @pl.when(jnp.logical_and(spot >= 0, spot < total.shape[0]))
            def _():
                total[spot] += grads[b].astype(jnp.float32)

        owned[...] = total[...].astype(jnp.bfloat16)


def spread(place, mixed, item, grads_in, grads_out, owned):
    vmem_spec = pl.BlockSpec(memory_space=pltpu.VMEM)
    shapes = [(owned,) + g.shape[1:] for g in (grads_in, grads_out)]
    return pl.pallas_call(
        spread_kernel,
        out_shape=tuple(
            jax.ShapeDtypeStruct(s, jnp.bfloat16) for s in (mixed.shape, item.shape, *shapes)
        ),
        in_specs=[pl.BlockSpec(memory_space=pltpu.SMEM)] + [vmem_spec] * 4,
        out_specs=(vmem_spec,) * 4,
        scratch_shapes=[pltpu.VMEM(s, jnp.float32) for s in shapes],
        name="spread",
    )(place, mixed, item, grads_in, grads_out)


def body(
    tokens,
    cotangent,
    gate_weight,
    up_weight,
    down_weight,
    block_task,
    block_fill,
    task_slot,
    inner_correction_weights,
    up_b,
):
    mixed, item, grads_in, grads_out, place = layer(
        tokens,
        cotangent,
        gate_weight,
        up_weight,
        down_weight,
        block_task,
        block_fill,
        task_slot,
        inner_correction_weights,
        up_b,
    )
    return spread(place, mixed, item, grads_in, grads_out, up_b.shape[0])


def solution(mesh):
    return jax.shard_map(
        body,
        mesh=mesh,
        in_specs=(
            P("dp", "tensor"),
            P("dp", "tensor"),
            P(None, "tensor"),
            P(None, "tensor"),
            P("tensor", None),
            P("dp"),
            P("dp"),
            P(),
            P("dp", None, "tensor"),
            P("dp", None, "tensor"),
        ),
        out_specs=(
            P("dp", "tensor"),
            P("dp", "tensor"),
            P("dp", None, "tensor"),
            P("dp", None, "tensor"),
        ),
        check_vma=False,
    )
```

```python
import functools

import jax
import jax.numpy as jnp
from jax import lax
from jax.experimental import pallas as pl
from jax.experimental.pallas import tpu as pltpu
from jax.sharding import PartitionSpec as P

BLOCK = 128
SIDE = 4
CHIPS = SIDE * SIDE
MESH = pl.DeviceIdType.MESH
COT = 1
LEND = 0
LOW = 9
HIDE = 18
MIX = 18
ITEM = 19
BEHIND = 3
SCATTER_BEHIND = 2
COMBINE = ((18, 15, 14, 11), (17, 15, 14, 13))
FINISH = ((21, 20, 19, 16), (20, 19, 18, 16))

GATHER_ORDER = (0, 4, 1, 8, 2, 12, 3, 5, 6, 10, 9, 13, 7, 14, 11, 15)
SCATTER_ORDER = (15, 12, 3, 14, 13, 11, 7, 10, 5, 9, 6, 8, 4, 2, 1, 0)

adapter_scale = 0.25


def packed(values, bits):
    word = sum(v << (bits * n) for n, v in enumerate(values))
    return jnp.int32(word - (1 << 32) if word >= 1 << 31 else word)


def pick(table, step):
    word = jnp.where(step < 8, packed(table[:8], 4), packed(table[8:], 4))
    return (word >> (4 * (step & 7))) & 15


def shifted(position, offset, sign):
    deltas = jnp.where(sign > 0, packed((0, 3, 1, 2), 2), packed((0, 1, 3, 2), 2))
    return (position + (deltas >> (2 * offset))) & 3


def timed(k, events):
    if not events:
        return
    steps = [e[0] for e in events]
    if steps[0] == steps[-1]:

        @pl.when(k == steps[0])
        def _():
            for _, do in events:
                do()

        return
    middle = steps[len(steps) // 2]
    if middle == steps[0]:
        middle = next(n for n in steps if n > middle)

    @pl.when(k < middle)
    def _():
        timed(k, [e for e in events if e[0] < middle])

    @pl.when(k >= middle)
    def _():
        timed(k, [e for e in events if e[0] >= middle])


def layer_kernel(
    tokens_ref,
    cotangent_ref,
    gate_hbm,
    up_hbm,
    down_hbm,
    task_ref,
    fill_ref,
    slot_ref,
    inner_hbm,
    up_b_hbm,
    mixed_ref,
    item_ref,
    grad_in_ref,
    grad_out_ref,
    place_ref,
    gathered,
    gate_up_w,
    down_w,
    gate_up,
    slope,
    dh_acc,
    hidden,
    d_both,
    d_up_ref,
    made,
    parts,
    landed,
    own_tokens,
    inner_own,
    up_b_own,
    task_tile,
    task_land,
    task_smem,
    lent_in,
    lent_out,
    borrowed_in,
    borrowed_out,
    inner_rows,
    up_rows,
    partial,
    sum_out,
    sum_in,
    low,
    grads_in,
    grads_out,
    landed_in,
    landed_out,
    own_sem,
    weight_sem,
    ag_send,
    ag_recv,
    pair_send,
    pair_recv,
    half_send,
    half_recv,
    rs_send,
    rs_recv,
    task_send,
    task_recv,
    lend_send,
    lend_recv,
    sum_send,
    sum_recv,
    grad_send,
    grad_recv,
    out_sem,
):
    rows, width = tokens_ref.shape
    blocks = rows // BLOCK
    part_rows = rows // 2
    hidden_width = hidden.shape[1]
    y = lax.axis_index("dp")
    owned_slots = inner_own.shape[0]
    me = lax.axis_index("tensor")
    core = me & 1
    x = (me >> 1) & 3
    z = me >> 3
    sign = 1 - 2 * core
    partner = me + sign

    here_columns = pl.ds(pl.multiple_of(core * width, width), width)
    there_columns = pl.ds(pl.multiple_of((1 - core) * width, width), width)
    my_chip = me >> 1

    def index(zz, xx, cc):
        return (zz * SIDE + xx) * 2 + cc

    x_up = index(z, (x + sign + SIDE) & 3, core)
    x_down = index(z, (x - sign + SIDE) & 3, core)
    z_up = index((z + sign + SIDE) & 3, x, core)
    z_down = index((z - sign + SIDE) & 3, x, core)
    along = {"x": (x_up, x_down), "z": (z_up, z_down)}

    def mine(idx):
        return shifted(z, idx & 3, sign) * SIDE + shifted(x, idx >> 2, sign)

    def theirs(idx):
        return shifted(z, idx & 3, -sign) * SIDE + shifted(x, idx >> 2, -sign)

    def remote(src, dst, send, recv, to):
        return pltpu.make_async_remote_copy(
            src_ref=src, dst_ref=dst, send_sem=send, recv_sem=recv, device_id={"tensor": to}, device_id_type=MESH
        )

    barrier = pltpu.get_barrier_semaphore()
    x_far = index(z, (x + 2) & 3, core)
    z_far = index((z + 2) & 3, x, core)
    for peer in (partner, x_up, x_down, z_up, z_down, x_far, z_far):
        pl.semaphore_signal(barrier, inc=1, device_id={"tensor": peer}, device_id_type=MESH)
    for d in (1, 2, 3):
        pl.semaphore_signal(barrier, inc=1, device_id={"dp": (y + d) & 3}, device_id_type=MESH)

    own = [
        pltpu.make_async_copy(ref, gathered.at[a, my_chip, :, here_columns], own_sem.at[a])
        for a, ref in enumerate((tokens_ref, cotangent_ref))
    ]
    for copy in own:
        copy.start()
    locals_in = (
        pltpu.make_async_copy(tokens_ref, own_tokens, own_sem.at[2]),
        pltpu.make_async_copy(inner_hbm, inner_own, own_sem.at[3]),
        pltpu.make_async_copy(up_b_hbm, up_b_own, own_sem.at[4]),
    )
    for copy in locals_in:
        copy.start()

    gate_part, up_part = slice(0, hidden_width), slice(hidden_width, 2 * hidden_width)

    def weight_copies(chip):
        at = pl.ds(pl.multiple_of(chip * 2 * width, 2 * width), 2 * width)
        return (
            pltpu.make_async_copy(gate_hbm.at[:, at], gate_up_w.at[chip, gate_part, :], weight_sem.at[0, chip]),
            pltpu.make_async_copy(up_hbm.at[:, at], gate_up_w.at[chip, up_part, :], weight_sem.at[1, chip]),
            pltpu.make_async_copy(down_hbm.at[:, at], down_w.at[chip], weight_sem.at[2, chip]),
        )

    lanes = lax.broadcasted_iota(jnp.int32, task_tile.shape, 1)
    tile = jnp.zeros(task_tile.shape, jnp.int32)
    for j in range(blocks):
        tile = jnp.where(lanes == j, task_ref[j], tile)
    task_tile[...] = tile

    pl.semaphore_wait(barrier, 10)

    def dp_remote(src, dst, send, recv, d):
        return pltpu.make_async_remote_copy(
            src_ref=src,
            dst_ref=dst,
            send_sem=send,
            recv_sem=recv,
            device_id={"dp": (y + d) & 3},
            device_id_type=MESH,
        )

    def task_copy(d):
        return dp_remote(task_tile, task_land.at[d - 1], task_send.at[d - 1], task_recv.at[d - 1], d)

    for d in (1, 2, 3):
        task_copy(d).start()

    half = (slice(0, part_rows), slice(part_rows, rows))

    def ag_copy(a, h, chip, idx, to):
        ref = gathered.at[a, chip, half[h], here_columns]
        return remote(ref, ref, ag_send.at[a, h, idx], ag_recv.at[a, h, idx], to)

    def arrive(a, idx, first):
        ox, oz = idx >> 2, idx & 3
        chip = mine(idx)
        if first:
            own[a].wait()
        for h, (name_f, name_g) in enumerate((("x", "z"), ("z", "x"))):
            of, og = (ox, oz) if h == 0 else (oz, ox)

            def spot(f, g, h=h):
                return f * SIDE + g if h == 0 else g * SIDE + f

            if not first:
                ag_copy(a, h, chip, idx, x_up).wait_recv()
            f_up, f_down = along[name_f]
            g_up, g_down = along[name_g]
            if first:
                ag_copy(a, h, chip, spot(1, 0), f_up).start()
                ag_copy(a, h, chip, spot(2, 0), f_down).start()
                ag_copy(a, h, chip, spot(0, 1), g_up).start()
                ag_copy(a, h, chip, spot(0, 2), g_down).start()
            else:

                @pl.when(jnp.logical_and(og == 0, of == 1))
                def _():
                    ag_copy(a, h, chip, spot(3, 0), f_up).start()

                @pl.when(og == 0)
                def _():
                    ag_copy(a, h, chip, spot(of, 1), g_up).start()
                    ag_copy(a, h, chip, spot(of, 2), g_down).start()

                @pl.when(og == 1)
                def _():
                    ag_copy(a, h, chip, spot(of, 3), g_up).start()

        pair_copy(a, chip, idx, here_columns).start()

    def pair_copy(a, chip, idx, columns):
        ref = gathered.at[a, chip, :, columns]
        return remote(ref, ref, pair_send.at[a, idx], pair_recv.at[a, idx], partner)

    arrive(0, jnp.int32(0), True)
    arrive(1, jnp.int32(0), True)

    def start_weights(k, carry):
        for copy in weight_copies(mine(pick(GATHER_ORDER, k))):
            copy.start()
        return carry

    lax.fori_loop(0, CHIPS, start_weights, 0)
    gate_up[...] = jnp.zeros_like(gate_up)
    dh_acc[...] = jnp.zeros_like(dh_acc)

    across = (((1,), (1,)), ((), ()))

    def lend_copy(kind, d):
        src, dst = ((lent_in, borrowed_in), (lent_out, borrowed_out))[kind]
        return dp_remote(src.at[d], dst.at[d - 1], lend_send.at[kind, d - 1], lend_recv.at[kind, d - 1], d)

    def spot_of(rank, j):
        task = task_smem[rank - 1, 0, j] if rank else task_ref[j]
        return slot_ref[task] - owned_slots * y

    def lend():
        for d in (1, 2, 3):
            task_copy(d).wait_recv()
        to_smem = pltpu.make_async_copy(task_land, task_smem, own_sem.at[5])
        to_smem.start()
        for copy in locals_in:
            copy.wait()
        to_smem.wait()
        for kind, (own_ref, lent) in enumerate(((inner_own, lent_in), (up_b_own, lent_out))):
            for d in (1, 2, 3, 0):
                for j in range(blocks):
                    spot = spot_of((SIDE - d) % SIDE, j)
                    held = jnp.logical_and(spot >= 0, spot < owned_slots)
                    safe = jnp.clip(spot, 0, owned_slots - 1)
                    factor = jnp.where(held, 1.0, 0.0)
                    lent[d, j] = (own_ref[safe].astype(jnp.float32) * factor).astype(jnp.bfloat16)
                if d:
                    lend_copy(kind, d).start()
        for d in range(SIDE):
            for j in range(blocks):
                place_ref[d * blocks + j] = spot_of(d, j)

    def borrow(kind):
        lent, borrowed, held = ((lent_in, borrowed_in, inner_rows), (lent_out, borrowed_out, up_rows))[kind]
        for d in (1, 2, 3):
            lend_copy(kind, d).wait_recv()
        held[...] = lent[0] + borrowed[0] + borrowed[1] + borrowed[2]

    def block_at(b):
        return slice(b * BLOCK, (b + 1) * BLOCK)

    rank_half = partial.shape[0] // 2
    here = pl.ds(pl.multiple_of(core * rank_half, rank_half), rank_half)
    there = pl.ds(pl.multiple_of((1 - core) * rank_half, rank_half), rank_half)

    def sum_copy(w, slot, src, to):
        return remote(sum_out.at[w, src], sum_in.at[w, slot], sum_send.at[w, slot], sum_recv.at[w, slot], to)

    def sum_pair(w):
        for b in range(blocks):
            if w == 0:
                left, right = inner_rows[b], own_tokens[block_at(b), :]
            else:
                left, right = up_rows[b], d_up_ref[block_at(b), :]
            partial[:, block_at(b)] = lax.dot_general(left, right, across, preferred_element_type=jnp.float32)
        sum_out[w, 0] = partial[there, :].astype(jnp.bfloat16)
        sum_copy(w, 0, 0, partner).start()

    def sum_x(w):
        sum_copy(w, 0, 0, partner).wait_recv()
        sum_out[w, 1] = (partial[here, :] + sum_in[w, 0].astype(jnp.float32)).astype(jnp.bfloat16)
        for d in (1, 2, 3):
            sum_copy(w, d, 1, index(z, (x + d) & 3, core)).start()

    def sum_four(w, own_slot, first):
        total = sum_out[w, own_slot].astype(jnp.float32)
        for d in range(3):
            sum_copy(w, first + d, own_slot, partner).wait_recv()
            total = total + sum_in[w, first + d].astype(jnp.float32)
        return total.astype(jnp.bfloat16)

    def sum_z(w):
        sum_out[w, 2] = sum_four(w, 1, 1)
        for d in (1, 2, 3):
            sum_copy(w, 3 + d, 2, index((z + d) & 3, x, core)).start()

    def sum_back(w):
        sum_out[w, 3] = sum_four(w, 2, 4)
        sum_copy(w, 7, 3, partner).start()

    def sum_end(w):
        sum_copy(w, 7, 3, partner).wait_recv()
        low[w, here, :] = sum_out[w, 3]
        low[w, there, :] = sum_in[w, 7]
        scale = (1.0, adapter_scale)[w]
        for b in range(blocks):
            live = lax.broadcasted_iota(jnp.int32, (2 * rank_half, BLOCK), 1) < fill_ref[b]
            value = low[w, :, block_at(b)].astype(jnp.float32)
            low[w, :, block_at(b)] = (scale * jnp.where(live, value, 0.0)).astype(jnp.bfloat16)

    def grad_copy(kind, d):
        src, dst = ((grads_in, landed_in), (grads_out, landed_out))[kind]
        return dp_remote(src, dst.at[d - 1], grad_send.at[kind, d - 1], grad_recv.at[kind, d - 1], d)

    def gradients(kind):
        for b in range(blocks):
            if kind == 0:
                grads_in[b] = jnp.dot(
                    low[1, :, block_at(b)], own_tokens[block_at(b), :], preferred_element_type=jnp.float32
                ).astype(jnp.bfloat16)
            else:
                grads_out[b] = (
                    adapter_scale
                    * jnp.dot(low[0, :, block_at(b)], d_up_ref[block_at(b), :], preferred_element_type=jnp.float32)
                ).astype(jnp.bfloat16)
        for d in (1, 2, 3):
            grad_copy(kind, d).start()
        out_copy(kind, 0).start()

    def out_copy(kind, d):
        ref, own_grads, landed_grads = ((grad_in_ref, grads_in, landed_in), (grad_out_ref, grads_out, landed_out))[kind]
        src = landed_grads.at[d - 1] if d else own_grads
        return pltpu.make_async_copy(src, ref.at[pl.ds(d * blocks, blocks)], out_sem.at[kind, d])

    def collect():
        for kind in (1, 0):
            for d in (1, 2, 3):
                grad_copy(kind, d).wait_recv()
                out_copy(kind, d).start()

    down_rank = (((0,), (0,)), ((), ()))

    def adjoint():
        for b in range(blocks):
            gate_up[block_at(b), 0:width] = lax.dot_general(
                low[1, :, block_at(b)], inner_rows[b], down_rank, preferred_element_type=jnp.float32
            )

    def use(a, chip):
        if a == 0:
            for copy in weight_copies(chip):
                copy.wait()
        total, weights = ((gate_up, gate_up_w), (dh_acc, down_w))[a]
        total[...] += lax.dot_general(
            gathered[a, chip], weights[chip], across, preferred_element_type=jnp.float32
        )

    def visit(a, k):
        @pl.when(jnp.logical_and(k >= 1, k < CHIPS))
        def _():
            arrive(a, pick(GATHER_ORDER, k), False)

        @pl.when(jnp.logical_and(k >= 1, k < CHIPS + 1))
        def _():
            idx = pick(GATHER_ORDER, k - 1)
            pair_copy(a, theirs(idx), idx, there_columns).wait_recv()

        @pl.when(k >= BEHIND)
        def _():
            use(a, mine(pick(GATHER_ORDER, k - BEHIND)))

    def hide():
        for b in range(blocks):
            slope[block_at(b), :] = adapter_scale * lax.dot_general(
                low[0, :, block_at(b)], up_rows[b], down_rank, preferred_element_type=jnp.float32
            )

        def some_rows(n, carry):
            at = pl.ds(pl.multiple_of(n * 64, 64), 64)
            gate = gate_up[at, gate_part]
            up = gate_up[at, up_part] + slope[at, :]
            sigmoid_gate = jax.nn.sigmoid(gate)
            activated = gate * sigmoid_gate
            hidden[at, :] = (activated * up).astype(jnp.bfloat16)
            gate_up[at, gate_part] = activated
            slope[at, :] = up * sigmoid_gate * (1.0 + gate * (1.0 - sigmoid_gate))
            return carry

        lax.fori_loop(0, rows // 64, some_rows, 0)

    def differentiate():
        def some_rows(n, carry):
            at = pl.ds(pl.multiple_of(n * 64, 64), 64)
            d_hidden = dh_acc[at, :]
            d_up = (d_hidden * gate_up[at, gate_part]).astype(jnp.bfloat16)
            d_both[at, gate_part] = (d_hidden * slope[at, :]).astype(jnp.bfloat16)
            d_both[at, up_part] = d_up
            d_up_ref[at, :] = d_up
            return carry

        lax.fori_loop(0, rows // 64, some_rows, 0)

    def product(r, chip):
        left, right = ((hidden, down_w), (d_both, gate_up_w))[r]
        return jnp.dot(left[...], right[chip], preferred_element_type=jnp.float32).astype(jnp.bfloat16)

    def mirrored(idx):
        swap = packed((0, 2, 1, 3), 2)
        return ((swap >> (2 * (idx >> 2))) & 3) * SIDE + ((swap >> (2 * (idx & 3))) & 3)

    def half_copy(r, slot, idx):
        to = mirrored(idx)
        return remote(
            made.at[r, slot, :, there_columns], parts.at[r, to], half_send.at[r, idx], half_recv.at[r, to], partner
        )

    def half_landed(r, idx):
        return remote(
            made.at[r, 0, :, there_columns], parts.at[r, idx], half_send.at[r, idx], half_recv.at[r, idx], partner
        )

    def rs_copy(r, h, idx, slot, to):
        return remote(parts.at[r, idx, half[h], :], landed.at[r, h, slot], rs_send.at[r, h, slot], rs_recv.at[r, h, slot], to)

    names = (("z", "x"), ("x", "z"))

    def place(h, f, g):
        return g * SIDE + f if h == 0 else f * SIDE + g

    def produce(r, k):
        @pl.when(k < CHIPS)
        def _():
            idx = pick(SCATTER_ORDER, k)
            slot = k & 3

            @pl.when(k >= 4)
            def _():
                half_copy(r, slot, pick(SCATTER_ORDER, k - 4)).wait_send()

            made[r, slot] = product(r, mine(idx))
            half_copy(r, slot, idx).start()

        @pl.when(k >= SCATTER_BEHIND)
        def _():
            idx = pick(SCATTER_ORDER, k - SCATTER_BEHIND)
            half_landed(r, idx).wait_recv()
            own_part = made[r, (k - SCATTER_BEHIND) & 3, :, here_columns].astype(jnp.float32)
            parts[r, idx] = (own_part + parts[r, idx].astype(jnp.float32)).astype(jnp.bfloat16)
            ox, oz = idx >> 2, idx & 3
            for h in (0, 1):
                of, og = (oz, ox) if h == 0 else (ox, oz)
                f_up, f_down = along[names[h][0]]

                @pl.when(of == 3)
                def _():
                    rs_copy(r, h, idx, og, f_down).start()

                @pl.when(of == 2)
                def _():
                    rs_copy(r, h, idx, SIDE + og, f_up).start()

    def add_in(r, h, idx, slots, out=None):
        for slot in slots:
            rs_copy(r, h, idx, slot, x_up).wait_recv()
        total = parts[r, idx, half[h], :].astype(jnp.float32)
        for slot in slots:
            total = total + landed[r, h, slot].astype(jnp.float32)
        if out is item_ref:
            total = total + gate_up[half[h], 0:width]
        if out is None:
            parts[r, idx, half[h], :] = total.astype(jnp.bfloat16)
        else:
            out[half[h], :] = total.astype(out.dtype)

    def combine(r, h, g):
        idx = place(h, 1, g)
        add_in(r, h, idx, (g,))
        rs_copy(r, h, idx, 2 * SIDE + g, along[names[h][0]][1]).start()

    def finish(r, h, g):
        idx = place(h, 0, g)
        add_in(r, h, idx, (SIDE + g, 2 * SIDE + g))
        g_up, g_down = along[names[h][1]]
        if g == 3:
            rs_copy(r, h, idx, 3 * SIDE, g_down).start()
        elif g == 2:
            rs_copy(r, h, idx, 3 * SIDE + 1, g_up).start()
        elif g == 1:
            add_in(r, h, idx, (3 * SIDE,))
            rs_copy(r, h, idx, 3 * SIDE + 2, g_down).start()
        else:
            add_in(r, h, idx, (3 * SIDE + 1, 3 * SIDE + 2), (mixed_ref, item_ref)[r])

    def both_halves(do, r, g):
        do(r, 0, g)
        do(r, 1, g)

    def drain():
        for d in (1, 2, 3):
            task_copy(d).wait_send()
            for kind in (0, 1):
                lend_copy(kind, d).wait_send()
                grad_copy(kind, d).wait_send()
        for w in (0, 1):
            for slot, src in enumerate((0, 1, 1, 1, 2, 2, 2, 3)):
                sum_copy(w, slot, src, partner).wait_send()
        for kind in (0, 1):
            for d in range(SIDE):
                out_copy(kind, d).wait()
        for k in range(CHIPS - 4, CHIPS):
            half_landed(0, SCATTER_ORDER[k]).wait_send()

        def one(k, carry):
            for a in (0, 1):
                pair_copy(a, my_chip, k, here_columns).wait_send()

                @pl.when(k >= 1)
                def _():
                    for h in (0, 1):
                        ag_copy(a, h, my_chip, k, x_up).wait_send()

            @pl.when(k < 15)
            def _():
                for h in (0, 1):
                    rs_copy(0, h, 0, k, x_up).wait_send()

            return carry

        lax.fori_loop(0, CHIPS, one, 0)

    early = [
        (LEND, lend),
        (LOW, lambda: borrow(0)),
        (LOW, lambda: sum_pair(0)),
        (LOW + 2, lambda: sum_x(0)),
        (LOW + 5, lambda: sum_z(0)),
        (LOW + 8, lambda: sum_back(0)),
        (HIDE, lambda: borrow(1)),
        (HIDE, lambda: sum_end(0)),
        (HIDE, hide),
        (ITEM, differentiate),
        (ITEM + 1, lambda: sum_pair(1)),
        (ITEM + 1, lambda: gradients(1)),
        (ITEM + 3, lambda: sum_x(1)),
        (ITEM + 6, lambda: sum_z(1)),
        (ITEM + 9, lambda: sum_back(1)),
        (ITEM + 12, lambda: sum_end(1)),
        (ITEM + 12, lambda: gradients(0)),
        (ITEM + 13, adjoint),
        (ITEM + FINISH[1][1], collect),
        (ITEM + FINISH[1][0], drain),
    ]
    late = []
    for r, start in ((0, MIX), (1, ITEM)):
        for g in (3, 2, 1, 0):
            late.append((start + COMBINE[r][g], functools.partial(both_halves, combine, r, g)))
            late.append((start + FINISH[r][g], functools.partial(both_halves, finish, r, g)))
    early.sort(key=lambda e: e[0])
    late.sort(key=lambda e: e[0])

    def step(k, carry):
        @pl.when(k < COT + CHIPS + BEHIND)
        def _():
            for a, start in ((0, 0), (1, COT)):

                @pl.when(jnp.logical_and(k >= start, k < start + CHIPS + BEHIND))
                def _():
                    visit(a, k - start)

        timed(k, early)

        @pl.when(k >= MIX)
        def _():
            for r, start in ((0, MIX), (1, ITEM)):

                @pl.when(jnp.logical_and(k >= start, k < start + CHIPS + SCATTER_BEHIND))
                def _():
                    produce(r, k - start)

            timed(k, late)

        return carry

    lax.fori_loop(0, max(MIX + FINISH[0][0], ITEM + FINISH[1][0]) + 1, step, 0)
    for k in range(CHIPS - 4, CHIPS):
        half_landed(1, SCATTER_ORDER[k]).wait_send()
    for h in (0, 1):
        for slot in range(15):
            rs_copy(1, h, 0, slot, x_up).wait_send()


def layer(
    tokens, cotangent, gate_weight, up_weight, down_weight, block_task, block_fill, task_slot, inner, up_b
):
    rows, width = tokens.shape
    hidden_width = gate_weight.shape[1]
    half = rows // 2
    blocks = rows // BLOCK
    owned, rank, _ = inner.shape
    any_spec = pl.BlockSpec(memory_space=pl.ANY)
    vmem_spec = pl.BlockSpec(memory_space=pltpu.VMEM)
    smem_spec = pl.BlockSpec(memory_space=pltpu.SMEM)
    bf16, f32 = jnp.bfloat16, jnp.float32
    dma = pltpu.SemaphoreType.DMA
    return pl.pallas_call(
        layer_kernel,
        out_shape=(
            jax.ShapeDtypeStruct((rows, width), bf16),
            jax.ShapeDtypeStruct((rows, width), bf16),
            jax.ShapeDtypeStruct((SIDE * blocks, rank, width), bf16),
            jax.ShapeDtypeStruct((SIDE * blocks, rank, hidden_width), bf16),
            jax.ShapeDtypeStruct((SIDE * blocks,), jnp.int32),
        ),
        in_specs=[any_spec] * 5 + [smem_spec] * 3 + [any_spec] * 2,
        out_specs=(vmem_spec, vmem_spec, any_spec, any_spec, smem_spec),
        scratch_shapes=[
            pltpu.VMEM((2, CHIPS, rows, 2 * width), bf16),
            pltpu.VMEM((CHIPS, 2 * hidden_width, 2 * width), bf16),
            pltpu.VMEM((CHIPS, hidden_width, 2 * width), bf16),
            pltpu.VMEM((rows, 2 * hidden_width), f32),
            pltpu.VMEM((rows, hidden_width), f32),
            pltpu.VMEM((rows, hidden_width), f32),
            pltpu.VMEM((rows, hidden_width), bf16),
            pltpu.VMEM((rows, 2 * hidden_width), bf16),
            pltpu.VMEM((rows, hidden_width), bf16),
            pltpu.VMEM((2, 4, rows, 2 * width), bf16),
            pltpu.VMEM((2, CHIPS, rows, width), bf16),
            pltpu.VMEM((2, 2, 15, half, width), bf16),
            pltpu.VMEM((rows, width), bf16),
            pltpu.VMEM((owned, rank, width), bf16),
            pltpu.VMEM((owned, rank, hidden_width), bf16),
            pltpu.VMEM((8, 128), jnp.int32),
            pltpu.VMEM((3, 8, 128), jnp.int32),
            pltpu.SMEM((3, 8, 128), jnp.int32),
            pltpu.VMEM((SIDE, blocks, rank, width), bf16),
            pltpu.VMEM((SIDE, blocks, rank, hidden_width), bf16),
            pltpu.VMEM((3, blocks, rank, width), bf16),
            pltpu.VMEM((3, blocks, rank, hidden_width), bf16),
            pltpu.VMEM((blocks, rank, width), bf16),
            pltpu.VMEM((blocks, rank, hidden_width), bf16),
            pltpu.VMEM((rank, rows), f32),
            pltpu.VMEM((2, 4, rank // 2, rows), bf16),
            pltpu.VMEM((2, 8, rank // 2, rows), bf16),
            pltpu.VMEM((2, rank, rows), bf16),
            pltpu.VMEM((blocks, rank, width), bf16),
            pltpu.VMEM((blocks, rank, hidden_width), bf16),
            pltpu.VMEM((3, blocks, rank, width), bf16),
            pltpu.VMEM((3, blocks, rank, hidden_width), bf16),
            dma((6,)),
            dma((3, CHIPS)),
            dma((2, 2, CHIPS)),
            dma((2, 2, CHIPS)),
            dma((2, CHIPS)),
            dma((2, CHIPS)),
            dma((2, CHIPS)),
            dma((2, CHIPS)),
            dma((2, 2, 15)),
            dma((2, 2, 15)),
            dma((3,)),
            dma((3,)),
            dma((2, 3)),
            dma((2, 3)),
            dma((2, 8)),
            dma((2, 8)),
            dma((2, 3)),
            dma((2, 3)),
            dma((2, SIDE)),
        ],
        compiler_params=pltpu.CompilerParams(
            collective_id=0, has_side_effects=True, vmem_limit_bytes=67043328
        ),
        name="layer",
    )(
        tokens,
        cotangent,
        gate_weight.T,
        up_weight.T,
        down_weight,
        block_task,
        block_fill,
        task_slot,
        inner,
        up_b,
    )


def spread_kernel(place_ref, mixed_in, item_in, grads_in, grads_out, mixed, item, owned_in, owned_out, sum_in, sum_out):
    mixed[...] = mixed_in[...]
    item[...] = item_in[...]
    for grads, total, owned in ((grads_in, sum_in, owned_in), (grads_out, sum_out, owned_out)):
        total[...] = jnp.zeros_like(total)

        @pl.loop(0, grads.shape[0])
        def _(b):
            spot = place_ref[b]

            @pl.when(jnp.logical_and(spot >= 0, spot < total.shape[0]))
            def _():
                total[spot] += grads[b].astype(jnp.float32)

        owned[...] = total[...].astype(jnp.bfloat16)


def spread(place, mixed, item, grads_in, grads_out, owned):
    vmem_spec = pl.BlockSpec(memory_space=pltpu.VMEM)
    shapes = [(owned,) + g.shape[1:] for g in (grads_in, grads_out)]
    return pl.pallas_call(
        spread_kernel,
        out_shape=tuple(
            jax.ShapeDtypeStruct(s, jnp.bfloat16) for s in (mixed.shape, item.shape, *shapes)
        ),
        in_specs=[pl.BlockSpec(memory_space=pltpu.SMEM)] + [vmem_spec] * 4,
        out_specs=(vmem_spec,) * 4,
        scratch_shapes=[pltpu.VMEM(s, jnp.float32) for s in shapes],
        name="spread",
    )(place, mixed, item, grads_in, grads_out)


def body(
    tokens,
    cotangent,
    gate_weight,
    up_weight,
    down_weight,
    block_task,
    block_fill,
    task_slot,
    inner_correction_weights,
    up_b,
):
    mixed, item, grads_in, grads_out, place = layer(
        tokens,
        cotangent,
        gate_weight,
        up_weight,
        down_weight,
        block_task,
        block_fill,
        task_slot,
        inner_correction_weights,
        up_b,
    )
    return spread(place, mixed, item, grads_in, grads_out, up_b.shape[0])


def solution(mesh):
    return jax.shard_map(
        body,
        mesh=mesh,
        in_specs=(
            P("dp", "tensor"),
            P("dp", "tensor"),
            P(None, "tensor"),
            P(None, "tensor"),
            P("tensor", None),
            P("dp"),
            P("dp"),
            P(),
            P("dp", None, "tensor"),
            P("dp", None, "tensor"),
        ),
        out_specs=(
            P("dp", "tensor"),
            P("dp", "tensor"),
            P("dp", None, "tensor"),
            P("dp", None, "tensor"),
        ),
        check_vma=False,
    )
```

```python
import functools

import jax
import jax.numpy as jnp
from jax import lax
from jax.experimental import pallas as pl
from jax.experimental.pallas import tpu as pltpu
from jax.sharding import PartitionSpec as P

BLOCK = 128
SIDE = 4
CHIPS = SIDE * SIDE
MESH = pl.DeviceIdType.MESH
COT = 1
LEND = 0
LOW = 9
HIDE = 18
MIX = 18
ITEM = 19
BEHIND = 3
SCATTER_BEHIND = 2
COMBINE = ((18, 14, 13, 9), (17, 15, 14, 13))
FINISH = ((21, 20, 18, 14), (20, 19, 18, 16))

GATHER_ORDER = (0, 4, 1, 8, 2, 12, 3, 5, 6, 10, 9, 13, 7, 14, 11, 15)
SCATTER_ORDER = (15, 12, 3, 14, 13, 11, 7, 10, 5, 9, 6, 8, 4, 2, 1, 0)

adapter_scale = 0.25


def packed(values, bits):
    word = sum(v << (bits * n) for n, v in enumerate(values))
    return jnp.int32(word - (1 << 32) if word >= 1 << 31 else word)


def pick(table, step):
    word = jnp.where(step < 8, packed(table[:8], 4), packed(table[8:], 4))
    return (word >> (4 * (step & 7))) & 15


def shifted(position, offset, sign):
    deltas = jnp.where(sign > 0, packed((0, 3, 1, 2), 2), packed((0, 1, 3, 2), 2))
    return (position + (deltas >> (2 * offset))) & 3


def timed(k, events):
    if not events:
        return
    steps = [e[0] for e in events]
    if steps[0] == steps[-1]:

        @pl.when(k == steps[0])
        def _():
            for _, do in events:
                do()

        return
    middle = steps[len(steps) // 2]
    if middle == steps[0]:
        middle = next(n for n in steps if n > middle)

    @pl.when(k < middle)
    def _():
        timed(k, [e for e in events if e[0] < middle])

    @pl.when(k >= middle)
    def _():
        timed(k, [e for e in events if e[0] >= middle])


def layer_kernel(
    tokens_ref,
    cotangent_ref,
    gate_hbm,
    up_hbm,
    down_hbm,
    task_ref,
    fill_ref,
    slot_ref,
    inner_hbm,
    up_b_hbm,
    mixed_ref,
    item_ref,
    grad_in_ref,
    grad_out_ref,
    place_ref,
    gathered,
    gate_up_w,
    down_w,
    gate_up,
    slope,
    dh_acc,
    hidden,
    d_both,
    d_up_ref,
    made,
    parts,
    landed,
    own_tokens,
    inner_own,
    up_b_own,
    task_tile,
    task_land,
    task_smem,
    lent_in,
    lent_out,
    borrowed_in,
    borrowed_out,
    inner_rows,
    up_rows,
    partial,
    sum_out,
    sum_in,
    low,
    grads_in,
    grads_out,
    landed_in,
    landed_out,
    own_sem,
    weight_sem,
    ag_send,
    ag_recv,
    pair_send,
    pair_recv,
    half_send,
    half_recv,
    rs_send,
    rs_recv,
    task_send,
    task_recv,
    lend_send,
    lend_recv,
    sum_send,
    sum_recv,
    grad_send,
    grad_recv,
    out_sem,
):
    rows, width = tokens_ref.shape
    blocks = rows // BLOCK
    part_rows = rows // 2
    hidden_width = hidden.shape[1]
    y = lax.axis_index("dp")
    owned_slots = inner_own.shape[0]
    me = lax.axis_index("tensor")
    core = me & 1
    x = (me >> 1) & 3
    z = me >> 3
    sign = 1 - 2 * core
    partner = me + sign

    here_columns = pl.ds(pl.multiple_of(core * width, width), width)
    there_columns = pl.ds(pl.multiple_of((1 - core) * width, width), width)
    my_chip = me >> 1

    def index(zz, xx, cc):
        return (zz * SIDE + xx) * 2 + cc

    x_up = index(z, (x + sign + SIDE) & 3, core)
    x_down = index(z, (x - sign + SIDE) & 3, core)
    z_up = index((z + sign + SIDE) & 3, x, core)
    z_down = index((z - sign + SIDE) & 3, x, core)
    along = {"x": (x_up, x_down), "z": (z_up, z_down)}

    def mine(idx):
        return shifted(z, idx & 3, sign) * SIDE + shifted(x, idx >> 2, sign)

    def theirs(idx):
        return shifted(z, idx & 3, -sign) * SIDE + shifted(x, idx >> 2, -sign)

    def remote(src, dst, send, recv, to):
        return pltpu.make_async_remote_copy(
            src_ref=src, dst_ref=dst, send_sem=send, recv_sem=recv, device_id={"tensor": to}, device_id_type=MESH
        )

    barrier = pltpu.get_barrier_semaphore()
    x_far = index(z, (x + 2) & 3, core)
    z_far = index((z + 2) & 3, x, core)
    for peer in (partner, x_up, x_down, z_up, z_down, x_far, z_far):
        pl.semaphore_signal(barrier, inc=1, device_id={"tensor": peer}, device_id_type=MESH)
    for d in (1, 2, 3):
        pl.semaphore_signal(barrier, inc=1, device_id={"dp": (y + d) & 3}, device_id_type=MESH)

    own = [
        pltpu.make_async_copy(ref, gathered.at[a, my_chip, :, here_columns], own_sem.at[a])
        for a, ref in enumerate((tokens_ref, cotangent_ref))
    ]
    for copy in own:
        copy.start()
    locals_in = (
        pltpu.make_async_copy(tokens_ref, own_tokens, own_sem.at[2]),
        pltpu.make_async_copy(inner_hbm, inner_own, own_sem.at[3]),
        pltpu.make_async_copy(up_b_hbm, up_b_own, own_sem.at[4]),
    )
    for copy in locals_in:
        copy.start()

    gate_part, up_part = slice(0, hidden_width), slice(hidden_width, 2 * hidden_width)

    def weight_copies(chip):
        at = pl.ds(pl.multiple_of(chip * 2 * width, 2 * width), 2 * width)
        return (
            pltpu.make_async_copy(gate_hbm.at[:, at], gate_up_w.at[chip, gate_part, :], weight_sem.at[0, chip]),
            pltpu.make_async_copy(up_hbm.at[:, at], gate_up_w.at[chip, up_part, :], weight_sem.at[1, chip]),
            pltpu.make_async_copy(down_hbm.at[:, at], down_w.at[chip], weight_sem.at[2, chip]),
        )

    lanes = lax.broadcasted_iota(jnp.int32, task_tile.shape, 1)
    tile = jnp.zeros(task_tile.shape, jnp.int32)
    for j in range(blocks):
        tile = jnp.where(lanes == j, task_ref[j], tile)
    task_tile[...] = tile

    pl.semaphore_wait(barrier, 10)

    def dp_remote(src, dst, send, recv, d):
        return pltpu.make_async_remote_copy(
            src_ref=src,
            dst_ref=dst,
            send_sem=send,
            recv_sem=recv,
            device_id={"dp": (y + d) & 3},
            device_id_type=MESH,
        )

    def task_copy(d):
        return dp_remote(task_tile, task_land.at[d - 1], task_send.at[d - 1], task_recv.at[d - 1], d)

    for d in (1, 2, 3):
        task_copy(d).start()

    half = (slice(0, part_rows), slice(part_rows, rows))

    def ag_copy(a, h, chip, idx, to):
        ref = gathered.at[a, chip, half[h], here_columns]
        return remote(ref, ref, ag_send.at[a, h, idx], ag_recv.at[a, h, idx], to)

    def arrive(a, idx, first):
        ox, oz = idx >> 2, idx & 3
        chip = mine(idx)
        if first:
            own[a].wait()
        for h, (name_f, name_g) in enumerate((("x", "z"), ("z", "x"))):
            of, og = (ox, oz) if h == 0 else (oz, ox)

            def spot(f, g, h=h):
                return f * SIDE + g if h == 0 else g * SIDE + f

            if not first:
                ag_copy(a, h, chip, idx, x_up).wait_recv()
            f_up, f_down = along[name_f]
            g_up, g_down = along[name_g]
            if first:
                ag_copy(a, h, chip, spot(1, 0), f_up).start()
                ag_copy(a, h, chip, spot(2, 0), f_down).start()
                ag_copy(a, h, chip, spot(0, 1), g_up).start()
                ag_copy(a, h, chip, spot(0, 2), g_down).start()
            else:

                @pl.when(jnp.logical_and(og == 0, of == 1))
                def _():
                    ag_copy(a, h, chip, spot(3, 0), f_up).start()

                @pl.when(og == 0)
                def _():
                    ag_copy(a, h, chip, spot(of, 1), g_up).start()
                    ag_copy(a, h, chip, spot(of, 2), g_down).start()

                @pl.when(og == 1)
                def _():
                    ag_copy(a, h, chip, spot(of, 3), g_up).start()

        pair_copy(a, chip, idx, here_columns).start()

    def pair_copy(a, chip, idx, columns):
        ref = gathered.at[a, chip, :, columns]
        return remote(ref, ref, pair_send.at[a, idx], pair_recv.at[a, idx], partner)

    arrive(0, jnp.int32(0), True)
    arrive(1, jnp.int32(0), True)

    def start_weights(k, carry):
        for copy in weight_copies(mine(pick(GATHER_ORDER, k))):
            copy.start()
        return carry

    lax.fori_loop(0, CHIPS, start_weights, 0)
    gate_up[...] = jnp.zeros_like(gate_up)
    dh_acc[...] = jnp.zeros_like(dh_acc)

    across = (((1,), (1,)), ((), ()))

    def lend_copy(kind, d):
        src, dst = ((lent_in, borrowed_in), (lent_out, borrowed_out))[kind]
        return dp_remote(src.at[d], dst.at[d - 1], lend_send.at[kind, d - 1], lend_recv.at[kind, d - 1], d)

    def spot_of(rank, j):
        task = task_smem[rank - 1, 0, j] if rank else task_ref[j]
        return slot_ref[task] - owned_slots * y

    def lend():
        for d in (1, 2, 3):
            task_copy(d).wait_recv()
        to_smem = pltpu.make_async_copy(task_land, task_smem, own_sem.at[5])
        to_smem.start()
        for copy in locals_in:
            copy.wait()
        to_smem.wait()
        for kind, (own_ref, lent) in enumerate(((inner_own, lent_in), (up_b_own, lent_out))):
            for d in (1, 2, 3, 0):
                for j in range(blocks):
                    spot = spot_of((SIDE - d) % SIDE, j)
                    held = jnp.logical_and(spot >= 0, spot < owned_slots)
                    safe = jnp.clip(spot, 0, owned_slots - 1)
                    factor = jnp.where(held, 1.0, 0.0)
                    lent[d, j] = (own_ref[safe].astype(jnp.float32) * factor).astype(jnp.bfloat16)
                if d:
                    lend_copy(kind, d).start()
        for d in range(SIDE):
            for j in range(blocks):
                place_ref[d * blocks + j] = spot_of(d, j)

    def borrow(kind):
        lent, borrowed, held = ((lent_in, borrowed_in, inner_rows), (lent_out, borrowed_out, up_rows))[kind]
        for d in (1, 2, 3):
            lend_copy(kind, d).wait_recv()
        held[...] = lent[0] + borrowed[0] + borrowed[1] + borrowed[2]

    def block_at(b):
        return slice(b * BLOCK, (b + 1) * BLOCK)

    rank_half = partial.shape[0] // 2
    here = pl.ds(pl.multiple_of(core * rank_half, rank_half), rank_half)
    there = pl.ds(pl.multiple_of((1 - core) * rank_half, rank_half), rank_half)

    def sum_copy(w, slot, src, to):
        return remote(sum_out.at[w, src], sum_in.at[w, slot], sum_send.at[w, slot], sum_recv.at[w, slot], to)

    def sum_pair(w):
        for b in range(blocks):
            if w == 0:
                left, right = inner_rows[b], own_tokens[block_at(b), :]
            else:
                left, right = up_rows[b], d_up_ref[block_at(b), :]
            partial[:, block_at(b)] = lax.dot_general(left, right, across, preferred_element_type=jnp.float32)
        sum_out[w, 0] = partial[there, :].astype(jnp.bfloat16)
        sum_copy(w, 0, 0, partner).start()

    def sum_x(w):
        sum_copy(w, 0, 0, partner).wait_recv()
        sum_out[w, 1] = (partial[here, :] + sum_in[w, 0].astype(jnp.float32)).astype(jnp.bfloat16)
        for d in (1, 2, 3):
            sum_copy(w, d, 1, index(z, (x + d) & 3, core)).start()

    def sum_four(w, own_slot, first):
        total = sum_out[w, own_slot].astype(jnp.float32)
        for d in range(3):
            sum_copy(w, first + d, own_slot, partner).wait_recv()
            total = total + sum_in[w, first + d].astype(jnp.float32)
        return total.astype(jnp.bfloat16)

    def sum_z(w):
        sum_out[w, 2] = sum_four(w, 1, 1)
        for d in (1, 2, 3):
            sum_copy(w, 3 + d, 2, index((z + d) & 3, x, core)).start()

    def sum_back(w):
        sum_out[w, 3] = sum_four(w, 2, 4)
        sum_copy(w, 7, 3, partner).start()

    def sum_end(w):
        sum_copy(w, 7, 3, partner).wait_recv()
        low[w, here, :] = sum_out[w, 3]
        low[w, there, :] = sum_in[w, 7]
        scale = (1.0, adapter_scale)[w]
        for b in range(blocks):
            live = lax.broadcasted_iota(jnp.int32, (2 * rank_half, BLOCK), 1) < fill_ref[b]
            value = low[w, :, block_at(b)].astype(jnp.float32)
            low[w, :, block_at(b)] = (scale * jnp.where(live, value, 0.0)).astype(jnp.bfloat16)

    def grad_copy(kind, d):
        src, dst = ((grads_in, landed_in), (grads_out, landed_out))[kind]
        return dp_remote(src, dst.at[d - 1], grad_send.at[kind, d - 1], grad_recv.at[kind, d - 1], d)

    def gradients(kind):
        for b in range(blocks):
            if kind == 0:
                grads_in[b] = jnp.dot(
                    low[1, :, block_at(b)], own_tokens[block_at(b), :], preferred_element_type=jnp.float32
                ).astype(jnp.bfloat16)
            else:
                grads_out[b] = (
                    adapter_scale
                    * jnp.dot(low[0, :, block_at(b)], d_up_ref[block_at(b), :], preferred_element_type=jnp.float32)
                ).astype(jnp.bfloat16)
        for d in (1, 2, 3):
            grad_copy(kind, d).start()
        out_copy(kind, 0).start()

    def out_copy(kind, d):
        ref, own_grads, landed_grads = ((grad_in_ref, grads_in, landed_in), (grad_out_ref, grads_out, landed_out))[kind]
        src = landed_grads.at[d - 1] if d else own_grads
        return pltpu.make_async_copy(src, ref.at[pl.ds(d * blocks, blocks)], out_sem.at[kind, d])

    def collect():
        for kind in (1, 0):
            for d in (1, 2, 3):
                grad_copy(kind, d).wait_recv()
                out_copy(kind, d).start()

    down_rank = (((0,), (0,)), ((), ()))

    def adjoint():
        for b in range(blocks):
            gate_up[block_at(b), 0:width] = lax.dot_general(
                low[1, :, block_at(b)], inner_rows[b], down_rank, preferred_element_type=jnp.float32
            )

    def use(a, chip):
        if a == 0:
            for copy in weight_copies(chip):
                copy.wait()
        total, weights = ((gate_up, gate_up_w), (dh_acc, down_w))[a]
        total[...] += lax.dot_general(
            gathered[a, chip], weights[chip], across, preferred_element_type=jnp.float32
        )

    def visit(a, k):
        @pl.when(jnp.logical_and(k >= 1, k < CHIPS))
        def _():
            arrive(a, pick(GATHER_ORDER, k), False)

        @pl.when(jnp.logical_and(k >= 1, k < CHIPS + 1))
        def _():
            idx = pick(GATHER_ORDER, k - 1)
            pair_copy(a, theirs(idx), idx, there_columns).wait_recv()

        @pl.when(k >= BEHIND)
        def _():
            use(a, mine(pick(GATHER_ORDER, k - BEHIND)))

    def hide():
        for b in range(blocks):
            slope[block_at(b), :] = adapter_scale * lax.dot_general(
                low[0, :, block_at(b)], up_rows[b], down_rank, preferred_element_type=jnp.float32
            )

        def some_rows(n, carry):
            at = pl.ds(pl.multiple_of(n * 64, 64), 64)
            gate = gate_up[at, gate_part]
            up = gate_up[at, up_part] + slope[at, :]
            sigmoid_gate = jax.nn.sigmoid(gate)
            activated = gate * sigmoid_gate
            hidden[at, :] = (activated * up).astype(jnp.bfloat16)
            gate_up[at, gate_part] = activated
            slope[at, :] = up * sigmoid_gate * (1.0 + gate * (1.0 - sigmoid_gate))
            return carry

        lax.fori_loop(0, rows // 64, some_rows, 0)

    def differentiate():
        def some_rows(n, carry):
            at = pl.ds(pl.multiple_of(n * 64, 64), 64)
            d_hidden = dh_acc[at, :]
            d_up = (d_hidden * gate_up[at, gate_part]).astype(jnp.bfloat16)
            d_both[at, gate_part] = (d_hidden * slope[at, :]).astype(jnp.bfloat16)
            d_both[at, up_part] = d_up
            d_up_ref[at, :] = d_up
            return carry

        lax.fori_loop(0, rows // 64, some_rows, 0)

    def product(r, chip):
        left, right = ((hidden, down_w), (d_both, gate_up_w))[r]
        return jnp.dot(left[...], right[chip], preferred_element_type=jnp.float32).astype(jnp.bfloat16)

    def mirrored(idx):
        swap = packed((0, 2, 1, 3), 2)
        return ((swap >> (2 * (idx >> 2))) & 3) * SIDE + ((swap >> (2 * (idx & 3))) & 3)

    def half_copy(r, slot, idx):
        to = mirrored(idx)
        return remote(
            made.at[r, slot, :, there_columns], parts.at[r, to], half_send.at[r, idx], half_recv.at[r, to], partner
        )

    def half_landed(r, idx):
        return remote(
            made.at[r, 0, :, there_columns], parts.at[r, idx], half_send.at[r, idx], half_recv.at[r, idx], partner
        )

    def rs_copy(r, h, idx, slot, to):
        return remote(parts.at[r, idx, half[h], :], landed.at[r, h, slot], rs_send.at[r, h, slot], rs_recv.at[r, h, slot], to)

    names = (("z", "x"), ("x", "z"))

    def place(h, f, g):
        return g * SIDE + f if h == 0 else f * SIDE + g

    def produce(r, k):
        @pl.when(k < CHIPS)
        def _():
            idx = pick(SCATTER_ORDER, k)
            slot = k & 3

            @pl.when(k >= 4)
            def _():
                half_copy(r, slot, pick(SCATTER_ORDER, k - 4)).wait_send()

            made[r, slot] = product(r, mine(idx))
            half_copy(r, slot, idx).start()

        @pl.when(k >= SCATTER_BEHIND)
        def _():
            idx = pick(SCATTER_ORDER, k - SCATTER_BEHIND)
            half_landed(r, idx).wait_recv()
            own_part = made[r, (k - SCATTER_BEHIND) & 3, :, here_columns].astype(jnp.float32)
            parts[r, idx] = (own_part + parts[r, idx].astype(jnp.float32)).astype(jnp.bfloat16)
            ox, oz = idx >> 2, idx & 3
            for h in (0, 1):
                of, og = (oz, ox) if h == 0 else (ox, oz)
                f_up, f_down = along[names[h][0]]

                @pl.when(of == 3)
                def _():
                    rs_copy(r, h, idx, og, f_down).start()

                @pl.when(of == 2)
                def _():
                    rs_copy(r, h, idx, SIDE + og, f_up).start()

    def add_in(r, h, idx, slots, out=None):
        for slot in slots:
            rs_copy(r, h, idx, slot, x_up).wait_recv()
        total = parts[r, idx, half[h], :].astype(jnp.float32)
        for slot in slots:
            total = total + landed[r, h, slot].astype(jnp.float32)
        if out is item_ref:
            total = total + gate_up[half[h], 0:width]
        if out is None:
            parts[r, idx, half[h], :] = total.astype(jnp.bfloat16)
        else:
            out[half[h], :] = total.astype(out.dtype)

    def combine(r, h, g):
        idx = place(h, 1, g)
        add_in(r, h, idx, (g,))
        rs_copy(r, h, idx, 2 * SIDE + g, along[names[h][0]][1]).start()

    def finish(r, h, g):
        idx = place(h, 0, g)
        add_in(r, h, idx, (SIDE + g, 2 * SIDE + g))
        g_up, g_down = along[names[h][1]]
        if g == 3:
            rs_copy(r, h, idx, 3 * SIDE, g_down).start()
        elif g == 2:
            rs_copy(r, h, idx, 3 * SIDE + 1, g_up).start()
        elif g == 1:
            add_in(r, h, idx, (3 * SIDE,))
            rs_copy(r, h, idx, 3 * SIDE + 2, g_down).start()
        else:
            add_in(r, h, idx, (3 * SIDE + 1, 3 * SIDE + 2), (mixed_ref, item_ref)[r])

    def both_halves(do, r, g):
        do(r, 0, g)
        do(r, 1, g)

    def drain():
        for d in (1, 2, 3):
            task_copy(d).wait_send()
            for kind in (0, 1):
                lend_copy(kind, d).wait_send()
                grad_copy(kind, d).wait_send()
        for w in (0, 1):
            for slot, src in enumerate((0, 1, 1, 1, 2, 2, 2, 3)):
                sum_copy(w, slot, src, partner).wait_send()
        for kind in (0, 1):
            for d in range(SIDE):
                out_copy(kind, d).wait()
        for k in range(CHIPS - 4, CHIPS):
            half_landed(0, SCATTER_ORDER[k]).wait_send()

        def one(k, carry):
            for a in (0, 1):
                pair_copy(a, my_chip, k, here_columns).wait_send()

                @pl.when(k >= 1)
                def _():
                    for h in (0, 1):
                        ag_copy(a, h, my_chip, k, x_up).wait_send()

            @pl.when(k < 15)
            def _():
                for h in (0, 1):
                    rs_copy(0, h, 0, k, x_up).wait_send()

            return carry

        lax.fori_loop(0, CHIPS, one, 0)

    early = [
        (LEND, lend),
        (LOW, lambda: borrow(0)),
        (LOW, lambda: sum_pair(0)),
        (LOW + 2, lambda: sum_x(0)),
        (LOW + 5, lambda: sum_z(0)),
        (LOW + 8, lambda: sum_back(0)),
        (HIDE, lambda: borrow(1)),
        (HIDE, lambda: sum_end(0)),
        (HIDE, hide),
        (ITEM, differentiate),
        (ITEM + 1, lambda: sum_pair(1)),
        (ITEM + 1, lambda: gradients(1)),
        (ITEM + 3, lambda: sum_x(1)),
        (ITEM + 6, lambda: sum_z(1)),
        (ITEM + 9, lambda: sum_back(1)),
        (ITEM + 12, lambda: sum_end(1)),
        (ITEM + 12, lambda: gradients(0)),
        (ITEM + 13, adjoint),
        (ITEM + FINISH[1][1], collect),
        (ITEM + FINISH[1][0], drain),
    ]
    late = []
    for r, start in ((0, MIX), (1, ITEM)):
        for g in (3, 2, 1, 0):
            late.append((start + COMBINE[r][g], functools.partial(both_halves, combine, r, g)))
            late.append((start + FINISH[r][g], functools.partial(both_halves, finish, r, g)))
    early.sort(key=lambda e: e[0])
    late.sort(key=lambda e: e[0])

    def step(k, carry):
        @pl.when(k < COT + CHIPS + BEHIND)
        def _():
            for a, start in ((0, 0), (1, COT)):

                @pl.when(jnp.logical_and(k >= start, k < start + CHIPS + BEHIND))
                def _():
                    visit(a, k - start)

        timed(k, early)

        @pl.when(k >= MIX)
        def _():
            for r, start in ((0, MIX), (1, ITEM)):

                @pl.when(jnp.logical_and(k >= start, k < start + CHIPS + SCATTER_BEHIND))
                def _():
                    produce(r, k - start)

            timed(k, late)

        return carry

    lax.fori_loop(0, max(MIX + FINISH[0][0], ITEM + FINISH[1][0]) + 1, step, 0)
    for k in range(CHIPS - 4, CHIPS):
        half_landed(1, SCATTER_ORDER[k]).wait_send()
    for h in (0, 1):
        for slot in range(15):
            rs_copy(1, h, 0, slot, x_up).wait_send()


def layer(
    tokens, cotangent, gate_weight, up_weight, down_weight, block_task, block_fill, task_slot, inner, up_b
):
    rows, width = tokens.shape
    hidden_width = gate_weight.shape[1]
    half = rows // 2
    blocks = rows // BLOCK
    owned, rank, _ = inner.shape
    any_spec = pl.BlockSpec(memory_space=pl.ANY)
    vmem_spec = pl.BlockSpec(memory_space=pltpu.VMEM)
    smem_spec = pl.BlockSpec(memory_space=pltpu.SMEM)
    bf16, f32 = jnp.bfloat16, jnp.float32
    dma = pltpu.SemaphoreType.DMA
    return pl.pallas_call(
        layer_kernel,
        out_shape=(
            jax.ShapeDtypeStruct((rows, width), bf16),
            jax.ShapeDtypeStruct((rows, width), bf16),
            jax.ShapeDtypeStruct((SIDE * blocks, rank, width), bf16),
            jax.ShapeDtypeStruct((SIDE * blocks, rank, hidden_width), bf16),
            jax.ShapeDtypeStruct((SIDE * blocks,), jnp.int32),
        ),
        in_specs=[any_spec] * 5 + [smem_spec] * 3 + [any_spec] * 2,
        out_specs=(vmem_spec, vmem_spec, any_spec, any_spec, smem_spec),
        scratch_shapes=[
            pltpu.VMEM((2, CHIPS, rows, 2 * width), bf16),
            pltpu.VMEM((CHIPS, 2 * hidden_width, 2 * width), bf16),
            pltpu.VMEM((CHIPS, hidden_width, 2 * width), bf16),
            pltpu.VMEM((rows, 2 * hidden_width), f32),
            pltpu.VMEM((rows, hidden_width), f32),
            pltpu.VMEM((rows, hidden_width), f32),
            pltpu.VMEM((rows, hidden_width), bf16),
            pltpu.VMEM((rows, 2 * hidden_width), bf16),
            pltpu.VMEM((rows, hidden_width), bf16),
            pltpu.VMEM((2, 4, rows, 2 * width), bf16),
            pltpu.VMEM((2, CHIPS, rows, width), bf16),
            pltpu.VMEM((2, 2, 15, half, width), bf16),
            pltpu.VMEM((rows, width), bf16),
            pltpu.VMEM((owned, rank, width), bf16),
            pltpu.VMEM((owned, rank, hidden_width), bf16),
            pltpu.VMEM((8, 128), jnp.int32),
            pltpu.VMEM((3, 8, 128), jnp.int32),
            pltpu.SMEM((3, 8, 128), jnp.int32),
            pltpu.VMEM((SIDE, blocks, rank, width), bf16),
            pltpu.VMEM((SIDE, blocks, rank, hidden_width), bf16),
            pltpu.VMEM((3, blocks, rank, width), bf16),
            pltpu.VMEM((3, blocks, rank, hidden_width), bf16),
            pltpu.VMEM((blocks, rank, width), bf16),
            pltpu.VMEM((blocks, rank, hidden_width), bf16),
            pltpu.VMEM((rank, rows), f32),
            pltpu.VMEM((2, 4, rank // 2, rows), bf16),
            pltpu.VMEM((2, 8, rank // 2, rows), bf16),
            pltpu.VMEM((2, rank, rows), bf16),
            pltpu.VMEM((blocks, rank, width), bf16),
            pltpu.VMEM((blocks, rank, hidden_width), bf16),
            pltpu.VMEM((3, blocks, rank, width), bf16),
            pltpu.VMEM((3, blocks, rank, hidden_width), bf16),
            dma((6,)),
            dma((3, CHIPS)),
            dma((2, 2, CHIPS)),
            dma((2, 2, CHIPS)),
            dma((2, CHIPS)),
            dma((2, CHIPS)),
            dma((2, CHIPS)),
            dma((2, CHIPS)),
            dma((2, 2, 15)),
            dma((2, 2, 15)),
            dma((3,)),
            dma((3,)),
            dma((2, 3)),
            dma((2, 3)),
            dma((2, 8)),
            dma((2, 8)),
            dma((2, 3)),
            dma((2, 3)),
            dma((2, SIDE)),
        ],
        compiler_params=pltpu.CompilerParams(
            collective_id=0, has_side_effects=True, vmem_limit_bytes=67043328
        ),
        name="layer",
    )(
        tokens,
        cotangent,
        gate_weight.T,
        up_weight.T,
        down_weight,
        block_task,
        block_fill,
        task_slot,
        inner,
        up_b,
    )


def spread_kernel(place_ref, mixed_in, item_in, grads_in, grads_out, mixed, item, owned_in, owned_out, sum_in, sum_out):
    mixed[...] = mixed_in[...]
    item[...] = item_in[...]
    for grads, total, owned in ((grads_in, sum_in, owned_in), (grads_out, sum_out, owned_out)):
        total[...] = jnp.zeros_like(total)

        @pl.loop(0, grads.shape[0])
        def _(b):
            spot = place_ref[b]

            @pl.when(jnp.logical_and(spot >= 0, spot < total.shape[0]))
            def _():
                total[spot] += grads[b].astype(jnp.float32)

        owned[...] = total[...].astype(jnp.bfloat16)


def spread(place, mixed, item, grads_in, grads_out, owned):
    vmem_spec = pl.BlockSpec(memory_space=pltpu.VMEM)
    shapes = [(owned,) + g.shape[1:] for g in (grads_in, grads_out)]
    return pl.pallas_call(
        spread_kernel,
        out_shape=tuple(
            jax.ShapeDtypeStruct(s, jnp.bfloat16) for s in (mixed.shape, item.shape, *shapes)
        ),
        in_specs=[pl.BlockSpec(memory_space=pltpu.SMEM)] + [vmem_spec] * 4,
        out_specs=(vmem_spec,) * 4,
        scratch_shapes=[pltpu.VMEM(s, jnp.float32) for s in shapes],
        name="spread",
    )(place, mixed, item, grads_in, grads_out)


def body(
    tokens,
    cotangent,
    gate_weight,
    up_weight,
    down_weight,
    block_task,
    block_fill,
    task_slot,
    inner_correction_weights,
    up_b,
):
    mixed, item, grads_in, grads_out, place = layer(
        tokens,
        cotangent,
        gate_weight,
        up_weight,
        down_weight,
        block_task,
        block_fill,
        task_slot,
        inner_correction_weights,
        up_b,
    )
    return spread(place, mixed, item, grads_in, grads_out, up_b.shape[0])


def solution(mesh):
    return jax.shard_map(
        body,
        mesh=mesh,
        in_specs=(
            P("dp", "tensor"),
            P("dp", "tensor"),
            P(None, "tensor"),
            P(None, "tensor"),
            P("tensor", None),
            P("dp"),
            P("dp"),
            P(),
            P("dp", None, "tensor"),
            P("dp", None, "tensor"),
        ),
        out_specs=(
            P("dp", "tensor"),
            P("dp", "tensor"),
            P("dp", None, "tensor"),
            P("dp", None, "tensor"),
        ),
        check_vma=False,
    )
```
